128 devices in a mesh: seq: 32 (over y, x, z_lo), head: 4 (over z_hi, core).
Axes of the slice: x: 4, y: 4, z: 4 (z_hi: 2, z_lo: 2; z = z_hi * 2 + z_lo), core: 2. Of those that a mesh axis runs over, the one named last changes fastest.
Arguments:
- queries: bfloat16 [8192, 2048], P('seq', 'head'), may hold values from -24 to 24
- key_vectors: bfloat16 [8192, 512], P('seq', 'head'), may hold values from -4 to 4
- values: bfloat16 [8192, 512], P('seq', 'head'), may hold values from -6 to 6
- out_proj: bfloat16 [2048, 4096], P('head'), may hold values from -0.125 to 0.125
- grad_out: bfloat16 [8192, 4096], P('seq', 'head'), may hold values from -6 to 6
- windows: int32 [16], P('head'), may hold values from 1024 to 2048, as said below
- slab_order: int32 [32], replicated, may hold values from 0 to 31, as said below
Outputs:
- layer_out: bfloat16 [8192, 4096], P('seq', 'head')
- grad_queries: bfloat16 [8192, 2048], P('seq', 'head')
- grad_keys: bfloat16 [8192, 512], P('seq', 'head')
- grad_values: bfloat16 [8192, 512], P('seq', 'head')
The draws below stay inside these ranges and needn't reach their ends.
Inputs may be any that keep to these rules, and one draw needn't show every extreme that they name: `windows`: some head's window is exactly 2048. slab_order[d] = (d + c) mod 32 for one c with 0 <= c < 32.
All inputs are finite; a program needn't handle non-finite values.
Results may differ from the reference program's by a relative error of at most 0.019.
Values may be sent and summed in bfloat16 or wider, within the bound.
A program may use at most 128 MiB of HBM per device.

```python
import jax
import jax.numpy as jnp
from jax import lax

MODEL_DIM = 4096
HEADS = 16
KV_HEADS = 4
HEAD_DIM = 128
TOK_DEV = 256
SLABS = 32
TOKENS = 8192
WIN_SLABS = 8
WINDOW = 2048
HEAD_SETS = 4


def drawn_pair(key):
    base = jax.random.fold_in(key, 7301)
    key_query, key_key = jax.random.split(base, 2)
    queries = 2.5 * jax.random.truncated_normal(key_query, -3.2, 3.2, (TOKENS, HEADS * HEAD_DIM), jnp.float32)
    key_vectors = jax.random.truncated_normal(key_key, -4.0, 4.0, (TOKENS, KV_HEADS * HEAD_DIM), jnp.float32)
    return (queries, key_vectors)


def draw_queries(key, part):
    return drawn_pair(key)[0].astype(jnp.bfloat16)


def draw_key_vectors(key, part):
    return drawn_pair(key)[1].astype(jnp.bfloat16)


def draw_windows(key, part):
    base = jax.random.fold_in(key, 4409)
    key_length, key_head = jax.random.split(base)
    lengths = jax.random.randint(key_length, (HEADS,), WINDOW // 2, WINDOW + 1)
    chosen = jax.random.randint(key_head, (), 0, HEADS)
    return jnp.where(jnp.arange(HEADS) == chosen, WINDOW, lengths).astype(jnp.int32)


def draw_slab_order(key, part):
    shift_by = jax.random.randint(jax.random.fold_in(key, 90211), (), 0, SLABS)
    return jnp.mod(jnp.arange(SLABS, dtype=jnp.int32) + shift_by, SLABS).astype(jnp.int32)


def shard_levels(own_key, extent, cuts, low, high):
    factor_of = 1.0
    for dim, shards_of in cuts:
        steps = jax.random.uniform(jax.random.fold_in(jax.random.fold_in(own_key, 6), dim), (shards_of,), jnp.float32, low / len(cuts), high / len(cuts))
        factor_of = factor_of * jnp.repeat(jnp.exp(steps), extent[dim] // shards_of).reshape((-1,) + (1,) * (len(extent) - 1 - dim))
    return factor_of


def scatter_about(rng, extent, deviation, bound, pieces=(), kind=jnp.bfloat16):
    factor_of = shard_levels(rng, extent, pieces, -0.22, 0.18) if pieces else 1.0
    values = jax.random.normal(rng, extent, jnp.float32) * deviation * factor_of
    return jnp.minimum(jnp.maximum(values, -bound), bound).astype(kind)


def setup_inputs(seed: int = 0) -> dict:
    streams_of = jax.random.split(jax.random.key(seed), 8)
    queries = draw_queries(jax.random.fold_in(streams_of[7], 71), 0)
    key_vectors = draw_key_vectors(jax.random.fold_in(streams_of[7], 71), 0)
    values = scatter_about(streams_of[2], (TOKENS, KV_HEADS * HEAD_DIM), 1.0, 6.0, ((0, 32), (1, 4)))
    out_proj = scatter_about(streams_of[3], (HEADS * HEAD_DIM, MODEL_DIM), (HEADS * HEAD_DIM) ** -0.5, 0.125, ((0, 4),))
    grad_out = scatter_about(streams_of[4], (TOKENS, MODEL_DIM), 1.0, 6.0, ((0, 32), (1, 4)))
    windows = draw_windows(jax.random.fold_in(streams_of[7], 71), 0)
    slab_order = draw_slab_order(jax.random.fold_in(streams_of[7], 71), 0)
    return {"queries": queries, "key_vectors": key_vectors, "values": values, "out_proj": out_proj, "grad_out": grad_out, "windows": windows, "slab_order": slab_order}


LOWEST = -1.0e30


def reference(queries, key_vectors, values, out_proj, grad_out, windows, slab_order):
    rows = TOK_DEV
    slabs = SLABS
    reach = WIN_SLABS
    span = (reach + 1) * rows
    groups = KV_HEADS
    ratio = HEADS // KV_HEADS
    scale = HEAD_DIM ** -0.5
    inverse = jnp.zeros((slabs,), jnp.int32).at[slab_order].set(jnp.arange(slabs, dtype=jnp.int32))

    def order(array):
        return array.reshape(slabs, rows, array.shape[1])[inverse].reshape(TOKENS, array.shape[1])

    def restore(array):
        return array.reshape(slabs, rows, array.shape[-1])[slab_order].reshape(TOKENS, array.shape[-1])

    grad_attn = jnp.dot(grad_out, out_proj.T, preferred_element_type=jnp.float32).astype(jnp.bfloat16)
    query_sorted = order(queries)
    grad_sorted = order(grad_attn)
    padding = jnp.zeros((reach * rows, groups * HEAD_DIM), jnp.bfloat16)
    key_padded = jnp.concatenate([padding, order(key_vectors)], 0)
    value_padded = jnp.concatenate([padding, order(values)], 0)
    spans = windows.reshape(groups, ratio)[:, :, None, None]
    offsets = jnp.arange(rows, dtype=jnp.int32)
    key_offsets = jnp.arange(span, dtype=jnp.int32)

    def one_slab(carry, slab):
        key_grads, value_grads = carry
        start = (slab * rows).astype(jnp.int32)
        query_heads = lax.dynamic_slice_in_dim(query_sorted, start, rows, 0).reshape(rows, groups, ratio, HEAD_DIM).astype(jnp.float32)
        grad_heads = lax.dynamic_slice_in_dim(grad_sorted, start, rows, 0).reshape(rows, groups, ratio, HEAD_DIM).astype(jnp.float32)
        key_heads = lax.dynamic_slice_in_dim(key_padded, start, span, 0).reshape(span, groups, HEAD_DIM).astype(jnp.float32)
        value_heads = lax.dynamic_slice_in_dim(value_padded, start, span, 0).reshape(span, groups, HEAD_DIM).astype(jnp.float32)
        query_place = start + offsets
        key_place = start - reach * rows + key_offsets
        distance = query_place[:, None] - key_place[None, :]
        mask = (distance >= 0) & (distance < spans) & (key_place >= 0)[None, :]
        scores = jnp.einsum("igrd,jgd->grij", query_heads, key_heads) * scale
        peak = jnp.max(jnp.where(mask, scores, LOWEST), -1)
        total = jnp.sum(jnp.exp(jnp.where(mask, scores - peak[..., None], LOWEST)), -1)
        log_norm = peak + jnp.log(total)
        probs = jnp.exp(jnp.where(mask, scores - log_norm[..., None], LOWEST))
        rounded = lax.optimization_barrier(probs.astype(jnp.bfloat16)).astype(jnp.float32)
        attention = jnp.einsum("grij,jgd->igrd", rounded, value_heads).astype(jnp.bfloat16)
        attention_wide = lax.optimization_barrier(attention).astype(jnp.float32)
        delta = jnp.einsum("igrd,igrd->gri", grad_heads, attention_wide)
        grad_prob = jnp.einsum("igrd,jgd->grij", grad_heads, value_heads)
        grad_score = (probs * (grad_prob - delta[..., None]) * scale).astype(jnp.bfloat16)
        grad_score = lax.optimization_barrier(grad_score).astype(jnp.float32)
        grad_q = jnp.einsum("grij,jgd->igrd", grad_score, key_heads)
        grad_k = jnp.einsum("grij,igrd->jgd", grad_score, query_heads).reshape(span, groups * HEAD_DIM)
        grad_v = jnp.einsum("grij,igrd->jgd", rounded, grad_heads).reshape(span, groups * HEAD_DIM)
        key_grads = lax.dynamic_update_slice_in_dim(key_grads, lax.dynamic_slice_in_dim(key_grads, start, span, 0) + grad_k, start, 0)
        value_grads = lax.dynamic_update_slice_in_dim(value_grads, lax.dynamic_slice_in_dim(value_grads, start, span, 0) + grad_v, start, 0)
        return (key_grads, value_grads), (attention.reshape(rows, HEADS * HEAD_DIM), grad_q.reshape(rows, HEADS * HEAD_DIM).astype(jnp.bfloat16))

    start_grads = jnp.zeros(((slabs + reach) * rows, groups * HEAD_DIM), jnp.float32)
    (key_grads, value_grads), (attention_sorted, grad_q_sorted) = lax.scan(one_slab, (start_grads, start_grads), jnp.arange(slabs, dtype=jnp.int32))
    attention = restore(attention_sorted)
    grad_queries = restore(grad_q_sorted)
    grad_keys = restore(key_grads[reach * rows:]).astype(jnp.bfloat16)
    grad_values = restore(value_grads[reach * rows:]).astype(jnp.bfloat16)
    width = HEADS * HEAD_DIM // HEAD_SETS
    summed = jnp.zeros((TOKENS, MODEL_DIM), jnp.float32)
    for member in range(HEAD_SETS):
        share = jnp.dot(attention[:, member * width:(member + 1) * width], out_proj[member * width:(member + 1) * width], preferred_element_type=jnp.float32)
        summed = summed + lax.optimization_barrier(share.astype(jnp.bfloat16)).astype(jnp.float32)
    layer_out = summed.astype(jnp.bfloat16)
    return layer_out, grad_queries, grad_keys, grad_values
```

```python
import jax
import jax.numpy as jnp
from jax import lax
from jax.experimental import pallas as pl
from jax.experimental.pallas import tpu as pltpu
from jax.sharding import PartitionSpec as P

MESH = pl.DeviceIdType.MESH
BF = jnp.bfloat16
F32 = jnp.float32
ROWS = 256
DIM = 128
RATIO = 4
SCALE = DIM ** (-0.5)
LOWEST = -1e30
OWN, SPARE = 8, 9


def nn(a, b):
    return jnp.dot(a, b, preferred_element_type=F32)


def nt(a, b):
    return lax.dot_general(a, b, (((1,), (1,)), ((), ())), preferred_element_type=F32)


def kernel(
    order, spans, q_hbm, k_hbm, v_hbm, w_hbm, g_hbm,
    out_ref, gq_ref, gk_ref, gv_ref,
    qv, kv, w, gb, qt, qs, st, peak, total, acc, gsum, dos, dot_t, lse, delta, dqt, attn,
    sh_send, sh_f0, sh_part, sh_opp, dsend, drecv, ysend, yrecv, dacc, place,
    lsem, c_send, c_recv, a_send, a_recv, b_send, b_recv, d_send, d_recv,
):
    s = lax.axis_index("seq")
    hd = lax.axis_index("head")
    y, x, zl = s // 8, (s // 2) % 4, s % 2
    zh, core = hd // 2, hd % 2
    r = 2 * x + zl
    rp = 2 * x + 1 - zl
    row0 = y * 8
    up = ((y + 1) % 4) * 8
    down = ((y + 3) % 4) * 8
    partner = {"head": 2 * zh + 1 - core}
    opposite = {"head": 2 * (1 - zh) + core}
    q0, q1 = 2 * zh + core, 2 * zh + 1 - core
    f0, f1 = 2 * (1 - zh) + core, 2 * (1 - zh) + 1 - core

    def at_seq(index):
        return {"seq": index}

    def remote(src, dst, send, recv, device):
        return pltpu.make_async_remote_copy(
            src_ref=src, dst_ref=dst, send_sem=send, recv_sem=recv, device_id=device, device_id_type=MESH
        )

    loads = [
        pltpu.make_async_copy(k_hbm, kv.at[OWN, pl.ds(0, ROWS)], lsem.at[0]),
        pltpu.make_async_copy(v_hbm, kv.at[OWN, pl.ds(ROWS, ROWS)], lsem.at[1]),
        pltpu.make_async_copy(g_hbm, gb.at[0], lsem.at[2]),
        pltpu.make_async_copy(q_hbm, qv, lsem.at[3]),
        pltpu.make_async_copy(w_hbm, w, lsem.at[4]),
    ]
    for load in loads:
        load.start()

    barrier = pltpu.get_barrier_semaphore()
    for away in range(1, 8):
        pl.semaphore_signal(barrier, inc=1, device_id=at_seq(row0 + (r + away) % 8), device_id_type=MESH)
    for device in (partner, opposite, at_seq(up + r), at_seq(down + r)):
        pl.semaphore_signal(barrier, inc=1, device_id=device, device_id_type=MESH)
    pl.semaphore_wait(barrier, 11)

    op_slot = jnp.where(zl == 0, SPARE, r - 1)
    yp_slot = jnp.where(zl == 0, r + 1, SPARE)
    op_there = jnp.where(zl == 1, SPARE, r)

    def kv_copy(src, dst, send, device):
        return remote(kv.at[src], kv.at[dst], c_send.at[send], c_recv.at[dst], device)

    def side(away, other):
        xx = (x + away) % 4
        later = xx > x
        if other:
            src = jnp.where(later, op_slot, yp_slot)
        else:
            src = jnp.where(later, OWN, r)
        dst = rp if other else r
        return later, kv_copy(src, dst, 3 + 2 * (away - 1) + other, at_seq(row0 + 2 * xx + zl))

    def start_sides(other, later_now):
        for away in (2, 1, 3):
            later, copy = side(away, other)

            @pl.when(later if later_now else jnp.logical_not(later))
            def _():
                copy.start()

    loads[0].wait()
    loads[1].wait()
    to_half = kv_copy(OWN, op_there, 0, at_seq(row0 + rp))
    to_half.start()
    to_up = kv_copy(OWN, r, 1, at_seq(up + r))
    to_up.start()
    start_sides(0, True)
    loads[2].wait()
    half = ROWS // 2
    a_opp = [
        remote(gb.at[0, pl.ds(i * half, half)], gb.at[2, pl.ds(i * half, half)], a_send.at[i], a_recv.at[i], opposite)
        for i in range(2)
    ]
    a_part = remote(gb.at[0], gb.at[1], a_send.at[2], a_recv.at[2], partner)
    a_fwd = [
        remote(gb.at[2, pl.ds(i * half, half)], gb.at[3, pl.ds(i * half, half)], a_send.at[3 + i], a_recv.at[3 + i], partner)
        for i in range(2)
    ]
    a_part.start()
    for copy in a_opp:
        copy.start()

    loads[3].wait()
    for h in range(RATIO):
        block = qv[:, h * DIM : (h + 1) * DIM]
        qs[pl.ds(h * ROWS, ROWS), :] = block
        qt[:, h * ROWS : (h + 1) * ROWS] = block.T
    place[...] = lax.broadcasted_iota(jnp.int32, (ROWS, ROWS), 1) - lax.broadcasted_iota(jnp.int32, (ROWS, ROWS), 0)

    mine = order[s]

    def forward(j, slot, hidden):
        key = kv[slot, pl.ds(0, ROWS), :]
        value_t = kv[slot, pl.ds(ROWS, ROWS), :].T
        for h in range(RATIO):
            cols = slice(h * ROWS, (h + 1) * ROWS)
            scores = jnp.where(hidden(h), LOWEST, nn(key, qt[:, cols]) * SCALE)
            st[j, :, cols] = scores
            top = jnp.max(scores, axis=0, keepdims=True)
            if hidden is causal:
                probs = jnp.exp(scores - top)
                peak[:, cols] = top
                total[:, cols] = jnp.sum(probs, axis=0, keepdims=True)
                acc[:, cols] = nn(value_t, probs.astype(BF))
            else:
                before = peak[:, cols]
                top = jnp.maximum(before, top)
                fade = jnp.exp(before - top)
                probs = jnp.exp(scores - top)
                peak[:, cols] = top
                total[:, cols] = total[:, cols] * fade + jnp.sum(probs, axis=0, keepdims=True)
                acc[:, cols] = acc[:, cols] * fade + nn(value_t, probs.astype(BF))

    def causal(h):
        return place[...] < 0

    def slot_of(j):
        pair = jnp.maximum(j - 3, 0) // 2
        away = 1 + 2 * pair - 3 * (pair // 2)
        parity = (zl + (j - 3) % 2) % 2
        return jnp.where(j == 1, rp, jnp.where(j == 2, r, 2 * ((x + away) % 4) + parity))

    def row_of(slot):
        return jnp.where(slot < r, row0, down)

    forward(0, OWN, causal)

    def await_slot(slot):
        kv_copy(OWN, slot, 0, at_seq(row0 + rp)).wait_recv()

    await_slot(op_slot)
    op_up = kv_copy(op_slot, yp_slot, 2, at_seq(up + r))
    op_up.start()
    start_sides(1, True)
    await_slot(r)
    start_sides(0, False)

    loads[4].wait()

    def w_cols(quarter):
        return pl.ds(pl.multiple_of(quarter * 1024, 1024), 1024)

    gsum[...] = nt(gb[0], w[:, w_cols(q0)])
    a_part.wait_recv()
    gsum[...] += nt(gb[1], w[:, w_cols(q1)])

    await_slot(yp_slot)
    start_sides(1, False)

    def forward_step(j, carry):
        slot = slot_of(j)

        @pl.when(j >= 3)
        def _():
            await_slot(slot)

        gap = (mine - order[row_of(slot) + slot]) * ROWS

        def windowed(h):
            limit = jnp.where(gap > 0, spans[h] - gap, -100000)
            return place[...] >= limit

        forward(j, slot, windowed)
        return carry

    lax.fori_loop(1, 9, forward_step, 0)

    for i in range(2):
        a_opp[i].wait_recv()
        a_fwd[i].start()

    norm = 1.0 / total[...]
    lse[...] = peak[...] + jnp.log(total[...])
    for h in range(RATIO):
        cols = slice(h * ROWS, (h + 1) * ROWS)
        mixed = (acc[:, cols] * norm[:, cols]).astype(BF)
        attn[:, h * DIM : (h + 1) * DIM] = mixed.T
        acc[:, cols] = mixed.astype(F32)

    def share(quarter):
        return nn(attn[...], w[:, w_cols(quarter)])

    sh_send[0] = share(f1).astype(BF)
    b_part = [remote(sh_send.at[i], sh_part.at[i], b_send.at[i], b_recv.at[i], partner) for i in range(2)]
    b_part[0].start()

    gsum[...] += nt(gb[2], w[:, w_cols(f0)])
    b_part[0].wait_recv()
    sh_f0[...] = (share(f0) + sh_part[0].astype(F32)).astype(BF)
    b_opp = remote(sh_f0, sh_opp, b_send.at[2], b_recv.at[2], opposite)
    b_opp.start()
    for copy in a_fwd:
        copy.wait_recv()
    gsum[...] += nt(gb[3], w[:, w_cols(f1)])
    for h in range(RATIO):
        cols = slice(h * ROWS, (h + 1) * ROWS)
        grad = gsum[:, h * DIM : (h + 1) * DIM].astype(BF)
        dos[pl.ds(h * ROWS, ROWS), :] = grad
        grad_t = grad.T
        dot_t[:, cols] = grad_t
        delta[:, cols] = jnp.sum(grad_t.astype(F32) * acc[:, cols], axis=0, keepdims=True)

    def backward(j, slot):
        key_t = kv[slot, pl.ds(0, ROWS), :].T
        value = kv[slot, pl.ds(ROWS, ROWS), :]
        probs_all = []
        grads_all = []
        for h in range(RATIO):
            cols = slice(h * ROWS, (h + 1) * ROWS)
            probs = jnp.exp(st[j, :, cols] - lse[:, cols])
            grad_probs = nn(value, dot_t[:, cols])
            probs_all.append(probs.astype(BF))
            grads_all.append((probs * (grad_probs - delta[:, cols])).astype(BF))
        probs_all = jnp.concatenate(probs_all, axis=1)
        grads_all = jnp.concatenate(grads_all, axis=1)
        grad_key = nn(grads_all, qs[...]) * SCALE
        grad_value = nn(probs_all, dos[...])
        dqt[...] += nn(key_t, grads_all)
        return grad_key, grad_value

    dqt[...] = jnp.zeros_like(dqt)

    def kv_grad_copy(slot):
        return remote(dsend.at[slot], drecv.at[r], d_send.at[slot], d_recv.at[r], at_seq(row0 + slot))

    def backward_step(i, carry):
        j = 8 - i
        slot = slot_of(j)
        grad_key, grad_value = backward(j, slot)

        @pl.when(j != 2)
        def _():
            dsend[slot, pl.ds(0, ROWS), :] = grad_key.astype(BF)
            dsend[slot, pl.ds(ROWS, ROWS), :] = grad_value.astype(BF)
            kv_grad_copy(slot).start()

        @pl.when(j == 2)
        def _():
            dacc[1, pl.ds(0, ROWS), :] = grad_key
            dacc[1, pl.ds(ROWS, ROWS), :] = grad_value

        return carry

    lax.fori_loop(0, 8, backward_step, 0)
    grad_key, grad_value = backward(0, OWN)
    dacc[0, pl.ds(0, ROWS), :] = grad_key
    dacc[0, pl.ds(ROWS, ROWS), :] = grad_value

    sh_send[1] = share(q1).astype(BF)
    b_part[1].start()
    for h in range(RATIO):
        gq_ref[:, h * DIM : (h + 1) * DIM] = (dqt[:, h * ROWS : (h + 1) * ROWS] * SCALE).astype(BF).T
    whole = share(q0)

    def add_from(index, which):
        remote(dsend.at[index], drecv.at[index], d_send.at[index], d_recv.at[index], at_seq(row0 + rp)).wait_recv()
        dacc[which] += drecv[index].astype(F32)

    @pl.loop(0, r)
    def _(index):
        add_from(index, 1)

    ysend[...] = dacc[1].astype(BF)
    y_copy = remote(ysend, yrecv, d_send.at[8], d_recv.at[8], at_seq(down + r))
    y_copy.start()

    @pl.loop(r + 1, 8)
    def _(index):
        add_from(index, 0)

    b_part[1].wait_recv()
    b_opp.wait_recv()
    out_ref[...] = (whole + sh_part[1].astype(F32) + sh_opp[...].astype(F32)).astype(BF)

    y_copy.wait_recv()
    final = dacc[0] + yrecv[...].astype(F32)
    gk_ref[...] = final[:ROWS].astype(BF)
    gv_ref[...] = final[ROWS:].astype(BF)

    for copy in (to_half, to_up, op_up, a_part, *a_opp, *a_fwd, *b_part, b_opp, y_copy):
        copy.wait_send()
    for away in (1, 2, 3):
        for other in (0, 1):
            side(away, other)[1].wait_send()
    for away in range(1, 8):
        kv_grad_copy((r + away) % 8).wait_send()


def body(queries, key_vectors, values, out_proj, grad_out, windows, slab_order):
    hbm = pl.BlockSpec(memory_space=pl.ANY)
    smem = pl.BlockSpec(memory_space=pltpu.SMEM)
    vmem = pl.BlockSpec(memory_space=pltpu.VMEM)
    wide = RATIO * ROWS
    return pl.pallas_call(
        kernel,
        name="layer",
        out_shape=(
            jax.ShapeDtypeStruct((ROWS, 1024), BF),
            jax.ShapeDtypeStruct((ROWS, RATIO * DIM), BF),
            jax.ShapeDtypeStruct((ROWS, DIM), BF),
            jax.ShapeDtypeStruct((ROWS, DIM), BF),
        ),
        in_specs=[smem, smem, hbm, hbm, hbm, hbm, hbm],
        out_specs=(vmem, vmem, vmem, vmem),
        scratch_shapes=[
            pltpu.VMEM((ROWS, RATIO * DIM), BF),
            pltpu.VMEM((10, 2 * ROWS, DIM), BF),
            pltpu.VMEM((RATIO * DIM, 4096), BF),
            pltpu.VMEM((4, ROWS, 1024), BF),
            pltpu.VMEM((DIM, wide), BF),
            pltpu.VMEM((wide, DIM), BF),
            pltpu.VMEM((9, ROWS, wide), F32),
            pltpu.VMEM((1, wide), F32),
            pltpu.VMEM((1, wide), F32),
            pltpu.VMEM((DIM, wide), F32),
            pltpu.VMEM((ROWS, RATIO * DIM), F32),
            pltpu.VMEM((wide, DIM), BF),
            pltpu.VMEM((DIM, wide), BF),
            pltpu.VMEM((1, wide), F32),
            pltpu.VMEM((1, wide), F32),
            pltpu.VMEM((DIM, wide), F32),
            pltpu.VMEM((ROWS, RATIO * DIM), BF),
            pltpu.VMEM((2, ROWS, 1024), BF),
            pltpu.VMEM((ROWS, 1024), BF),
            pltpu.VMEM((2, ROWS, 1024), BF),
            pltpu.VMEM((ROWS, 1024), BF),
            pltpu.VMEM((8, 2 * ROWS, DIM), BF),
            pltpu.VMEM((8, 2 * ROWS, DIM), BF),
            pltpu.VMEM((2 * ROWS, DIM), BF),
            pltpu.VMEM((2 * ROWS, DIM), BF),
            pltpu.VMEM((2, 2 * ROWS, DIM), F32),
            pltpu.VMEM((ROWS, ROWS), jnp.int32),
            pltpu.SemaphoreType.DMA((5,)),
            pltpu.SemaphoreType.DMA((9,)),
            pltpu.SemaphoreType.DMA((10,)),
            pltpu.SemaphoreType.DMA((5,)),
            pltpu.SemaphoreType.DMA((5,)),
            pltpu.SemaphoreType.DMA((3,)),
            pltpu.SemaphoreType.DMA((3,)),
            pltpu.SemaphoreType.DMA((9,)),
            pltpu.SemaphoreType.DMA((9,)),
        ],
        compiler_params=pltpu.CompilerParams(collective_id=0, has_side_effects=True, vmem_limit_bytes=56 * 1024 * 1024),
    )(slab_order, windows, queries, key_vectors, values, out_proj, grad_out)


def solution(mesh):
    in_specs = (
        P("seq", "head"),
        P("seq", "head"),
        P("seq", "head"),
        P("head", None),
        P("seq", "head"),
        P("head"),
        P(),
    )
    out_specs = (P("seq", "head"), P("seq", "head"), P("seq", "head"), P("seq", "head"))
    return jax.shard_map(body, mesh=mesh, in_specs=in_specs, out_specs=out_specs, check_vma=False)
```

```python
import jax
import jax.numpy as jnp
from jax import lax
from jax.experimental import pallas as pl
from jax.experimental.pallas import tpu as pltpu
from jax.sharding import PartitionSpec as P

MESH = pl.DeviceIdType.MESH
BF = jnp.bfloat16
F32 = jnp.float32
ROWS = 256
DIM = 128
RATIO = 4
SCALE = DIM ** (-0.5)
LOG2E = 1.4426950408889634
LOWEST = -1e30
OWN, SPARE = 8, 9


def nn(a, b):
    return jnp.dot(a, b, preferred_element_type=F32)


def nt(a, b):
    return lax.dot_general(a, b, (((1,), (1,)), ((), ())), preferred_element_type=F32)


def kernel(
    order, spans, q_hbm, k_hbm, v_hbm, w_hbm, g_hbm,
    out_ref, gq_ref, gk_ref, gv_ref,
    qv, kv, w, gb, qt, qs, st, peak, total, acc, gsum, dos, dot_t, lse, delta, dqt, attn,
    sh_send, sh_f0, sh_part, sh_opp, dsend, drecv, ysend, yrecv, zsend, zrecv, dacc, place,
    lsem, c_send, c_recv, a_send, a_recv, b_send, b_recv, d_send, d_recv, y_send, y_recv, z_send, z_recv,
):
    s = lax.axis_index("seq")
    hd = lax.axis_index("head")
    y, x, zl = s // 8, (s // 2) % 4, s % 2
    zh, core = hd // 2, hd % 2
    r = 2 * x + zl
    rp = 2 * x + 1 - zl
    row0 = y * 8
    up = ((y + 1) % 4) * 8
    down = ((y + 3) % 4) * 8
    partner = {"head": 2 * zh + 1 - core}
    opposite = {"head": 2 * (1 - zh) + core}
    q0, q1 = 2 * zh + core, 2 * zh + 1 - core
    f0, f1 = 2 * (1 - zh) + core, 2 * (1 - zh) + 1 - core

    def at_seq(index):
        return {"seq": index}

    def remote(src, dst, send, recv, device):
        return pltpu.make_async_remote_copy(
            src_ref=src, dst_ref=dst, send_sem=send, recv_sem=recv, device_id=device, device_id_type=MESH
        )

    loads = [
        pltpu.make_async_copy(k_hbm, kv.at[OWN, 0], lsem.at[0]),
        pltpu.make_async_copy(v_hbm, kv.at[OWN, 1], lsem.at[1]),
        pltpu.make_async_copy(g_hbm, gb.at[0], lsem.at[2]),
        pltpu.make_async_copy(q_hbm, qv, lsem.at[3]),
        pltpu.make_async_copy(w_hbm, w, lsem.at[4]),
    ]
    for load in loads:
        load.start()

    barrier = pltpu.get_barrier_semaphore()
    for away in range(1, 4):
        pl.semaphore_signal(barrier, inc=1, device_id=at_seq(row0 + (r + 2 * away) % 8), device_id_type=MESH)
    for device in (at_seq(row0 + rp), partner, opposite, at_seq(up + r), at_seq(down + r)):
        pl.semaphore_signal(barrier, inc=1, device_id=device, device_id_type=MESH)
    place[...] = lax.broadcasted_iota(jnp.int32, (ROWS, ROWS), 1) - lax.broadcasted_iota(jnp.int32, (ROWS, ROWS), 0)
    dqt[...] = jnp.zeros_like(dqt)
    dacc[zl, 1] = jnp.zeros((2, ROWS, DIM), F32)
    loads[3].wait()
    for h in range(RATIO):
        block = qv[:, h * DIM : (h + 1) * DIM]
        qs[pl.ds(h * ROWS, ROWS), :] = block
        qt[:, h * ROWS : (h + 1) * ROWS] = block.T
    for i in range(3):
        loads[i].wait()
    pl.semaphore_wait(barrier, 8)

    op_slot = jnp.where(zl == 0, SPARE, r - 1)
    yp_slot = jnp.where(zl == 0, r + 1, SPARE)
    op_there = jnp.where(zl == 1, SPARE, r)

    def kv_copy(src, dst, part, send, device):
        return remote(kv.at[src, part], kv.at[dst, part], c_send.at[send, part], c_recv.at[dst, part], device)

    def side(away, other, part):
        xx = (x + away) % 4
        later = xx > x
        if other:
            src = jnp.where(later, op_slot, yp_slot)
        else:
            src = jnp.where(later, OWN, r)
        dst = rp if other else r
        return later, kv_copy(src, dst, part, 3 + 2 * (away - 1) + other, at_seq(row0 + 2 * xx + zl))

    def start_sides(other, later_now, part):
        for away in (2, 1, 3):
            later, copy = side(away, other, part)

            @pl.when(later if later_now else jnp.logical_not(later))
            def _():
                copy.start()

    def to_half(part):
        return kv_copy(OWN, op_there, part, 0, at_seq(row0 + rp))

    def to_up(part):
        return kv_copy(OWN, r, part, 1, at_seq(up + r))

    def op_up(part):
        return kv_copy(op_slot, yp_slot, part, 2, at_seq(up + r))

    def await_part(slot, part):
        kv_copy(OWN, slot, part, 0, at_seq(row0 + rp)).wait_recv()

    for part in (0, 1):
        to_half(part).start()
        to_up(part).start()
    for part in (0, 1):
        start_sides(0, True, part)
    half = ROWS // 2
    a_opp = [
        remote(gb.at[0, pl.ds(i * half, half)], gb.at[2, pl.ds(i * half, half)], a_send.at[i], a_recv.at[i], opposite)
        for i in range(2)
    ]
    a_part = remote(gb.at[0], gb.at[1], a_send.at[2], a_recv.at[2], partner)
    a_fwd = [
        remote(gb.at[2, pl.ds(i * half, half)], gb.at[3, pl.ds(i * half, half)], a_send.at[3 + i], a_recv.at[3 + i], partner)
        for i in range(2)
    ]
    a_part.start()
    for copy in a_opp:
        copy.start()

    mine = order[s]

    def forward(slot, hidden, first=False):
        key = kv[slot, 0]
        value_t = kv[slot, 1].T
        tops = []
        for h in range(RATIO):
            cols = slice(h * ROWS, (h + 1) * ROWS)
            scores = jnp.where(hidden(h), LOWEST, nn(key, qt[:, cols]) * (SCALE * LOG2E))
            st[slot, :, cols] = scores
            tops.append(jnp.max(scores, axis=0, keepdims=True))
        for h in range(RATIO):
            cols = slice(h * ROWS, (h + 1) * ROWS)
            if first:
                top = tops[h]
                probs = jnp.exp2(st[slot, :, cols] - top)
                total[:, cols] = jnp.sum(probs, axis=0, keepdims=True)
                acc[:, cols] = nn(value_t, probs.astype(BF))
            else:
                before = peak[:, cols]
                top = jnp.maximum(before, tops[h])
                fade = jnp.exp2(before - top)
                probs = jnp.exp2(st[slot, :, cols] - top)
                total[:, cols] = total[:, cols] * fade + jnp.sum(probs, axis=0, keepdims=True)
                acc[:, cols] = acc[:, cols] * fade + nn(value_t, probs.astype(BF))
            peak[:, cols] = top

    def forward_on(slot):
        row = jnp.where(slot < r, row0, down)
        gap = (mine - order[row + slot]) * ROWS

        def windowed(h):
            limit = jnp.where(gap > 0, spans[h] - gap, -100000)
            return place[...] >= limit

        forward(slot, windowed)

    def pair_slot(away, other):
        return 2 * ((x + away) % 4) + (zl + other) % 2

    forward(OWN, lambda h: place[...] < 0, first=True)

    for part in (0, 1):
        await_part(op_slot, part)
        op_up(part).start()
        start_sides(1, True, part)
    for part in (0, 1):
        await_part(r, part)
        start_sides(0, False, part)
    forward_on(r)

    loads[4].wait()

    def w_cols(quarter):
        return pl.ds(pl.multiple_of(quarter * 1024, 1024), 1024)

    gsum[...] = nt(gb[0], w[:, w_cols(q0)])
    a_part.wait_recv()
    gsum[...] += nt(gb[1], w[:, w_cols(q1)])

    for part in (0, 1):
        await_part(yp_slot, part)
        start_sides(1, False, part)
    forward_on(rp)

    def forward_step(j, carry):
        away = 3 - 2 * (j % 3) + 3 * ((j % 3) // 2)
        slot = pair_slot(away, j // 3)
        for part in (0, 1):
            await_part(slot, part)
        forward_on(slot)
        return carry

    lax.fori_loop(0, 5, forward_step, 0)
    a_opp[0].wait_recv()
    a_fwd[0].start()
    lax.fori_loop(5, 6, forward_step, 0)
    a_opp[1].wait_recv()
    a_fwd[1].start()

    norm = 1.0 / total[...]
    lse[...] = peak[...] + jnp.log(total[...]) * LOG2E
    for h in range(RATIO):
        cols = slice(h * ROWS, (h + 1) * ROWS)
        mixed = (acc[:, cols] * norm[:, cols]).astype(BF)
        attn[:, h * DIM : (h + 1) * DIM] = mixed.T
        acc[:, cols] = mixed.astype(F32)

    def share(quarter):
        return nn(attn[...], w[:, w_cols(quarter)])

    sh_send[0] = share(f1).astype(BF)
    b_part = [remote(sh_send.at[i], sh_part.at[i], b_send.at[i], b_recv.at[i], partner) for i in range(2)]
    b_part[0].start()

    gsum[...] += nt(gb[2], w[:, w_cols(f0)])
    for copy in a_fwd:
        copy.wait_recv()
    gsum[...] += nt(gb[3], w[:, w_cols(f1)])
    for h in range(RATIO):
        cols = slice(h * ROWS, (h + 1) * ROWS)
        grad = gsum[:, h * DIM : (h + 1) * DIM].astype(BF)
        dos[pl.ds(h * ROWS, ROWS), :] = grad
        grad_t = grad.T
        dot_t[:, cols] = grad_t
        delta[:, cols] = jnp.sum(grad_t.astype(F32) * acc[:, cols], axis=0, keepdims=True)

    def backward(slot):
        key_t = kv[slot, 0].T
        value = kv[slot, 1]
        probs_all = []
        grads_all = []
        for h in range(RATIO):
            cols = slice(h * ROWS, (h + 1) * ROWS)
            probs = jnp.exp2(st[slot, :, cols] - lse[:, cols])
            grad_probs = nn(value, dot_t[:, cols])
            probs_all.append(probs.astype(BF))
            grads_all.append((probs * (grad_probs - delta[:, cols])).astype(BF))
        probs_all = jnp.concatenate(probs_all, axis=1)
        grads_all = jnp.concatenate(grads_all, axis=1)
        grad_key = nn(grads_all, qs[...]) * SCALE
        grad_value = nn(probs_all, dos[...])
        dqt[...] += nn(key_t, grads_all)
        return grad_key, grad_value

    def pair_grads(away, other):
        slot = pair_slot(away, other)
        return remote(
            dsend.at[slot], drecv.at[x, other], d_send.at[slot], d_recv.at[x, other], at_seq(row0 + 2 * ((x + away) % 4) + zl)
        )

    def backward_step(j, carry):
        away, other = 1 + j // 2, 1 - j % 2
        slot = pair_slot(away, other)
        grad_key, grad_value = backward(slot)
        dsend[slot, 0] = grad_key.astype(BF)
        dsend[slot, 1] = grad_value.astype(BF)
        pair_grads(away, other).start()
        return carry

    lax.fori_loop(0, 2, backward_step, 0)
    b_part[0].wait_recv()
    sh_f0[...] = (share(f0) + sh_part[0].astype(F32)).astype(BF)
    b_opp = remote(sh_f0, sh_opp, b_send.at[2], b_recv.at[2], opposite)
    b_opp.start()
    lax.fori_loop(2, 6, backward_step, 0)

    def backward_here(slot, row, other):
        grad_key, grad_value = backward(slot)
        dacc[row, other, 0] = grad_key
        dacc[row, other, 1] = grad_value

    backward_here(rp, 1 - zl, 1)
    backward_here(r, 1, 0)

    def pair_from(index, other):
        return remote(dsend.at[r], drecv.at[index, other], d_send.at[r], d_recv.at[index, other], at_seq(row0 + rp))

    def y_copy(other, part):
        return remote(
            ysend.at[other, part], yrecv.at[other, part], y_send.at[other, part], y_recv.at[other, part], at_seq(down + r)
        )

    def z_copy(part):
        return remote(zsend.at[part], zrecv.at[part], z_send.at[part], z_recv.at[part], at_seq(row0 + rp))

    def add_from(index, row, other):
        pair_from(index, other).wait_recv()
        dacc[row, other] += drecv[index, other].astype(F32)

    def send_up(other):
        @pl.loop(0, x)
        def _(index):
            add_from(x - 1 - index, 1, other)

        for part in (0, 1):
            ysend[other, part] = dacc[1, other, part].astype(BF)
            y_copy(other, part).start()

    has_other = x + 1 - zl > 0
    backward_here(OWN, 0, 0)
    sh_send[1] = share(q1).astype(BF)
    b_part[1].start()
    for h in range(RATIO):
        gq_ref[:, h * DIM : (h + 1) * DIM] = (dqt[:, h * ROWS : (h + 1) * ROWS] * SCALE).astype(BF).T
    whole = share(q0)
    b_part[1].wait_recv()
    gsum_wide = whole + sh_part[1].astype(F32)

    @pl.when(has_other)
    def _():
        send_up(1)

    send_up(0)

    @pl.loop(x + 1, 4)
    def _(index):
        add_from(index, 0, 1)
        add_from(index, 0, 0)

    b_opp.wait_recv()
    out_ref[...] = (gsum_wide + sh_opp[...].astype(F32)).astype(BF)

    for part in (0, 1):

        @pl.when(has_other)
        def _():
            y_copy(1, part).wait_recv()
            zsend[part] = (dacc[0, 1, part] + yrecv[1, part].astype(F32)).astype(BF)

        @pl.when(jnp.logical_not(has_other))
        def _():
            zsend[part] = dacc[0, 1, part].astype(BF)

        z_copy(part).start()

    for part, result in ((0, gk_ref), (1, gv_ref)):
        y_copy(0, part).wait_recv()
        z_copy(part).wait_recv()
        result[...] = (dacc[0, 0, part] + yrecv[0, part].astype(F32) + zrecv[part].astype(F32)).astype(BF)

    for part in (0, 1):
        for copy in (to_half(part), to_up(part), op_up(part), y_copy(0, part), z_copy(part)):
            copy.wait_send()
        for away in (1, 2, 3):
            for other in (0, 1):
                side(away, other, part)[1].wait_send()

        @pl.when(has_other)
        def _():
            y_copy(1, part).wait_send()

    for copy in (a_part, *a_opp, *a_fwd, *b_part, b_opp):
        copy.wait_send()
    for away in (1, 2, 3):
        for other in (0, 1):
            pair_grads(away, other).wait_send()


def finish(*refs):
    ins, outs, sems = refs[:4], refs[4:8], refs[8]
    copies = [pltpu.make_async_copy(a, b, sems.at[i]) for i, (a, b) in enumerate(zip(ins, outs))]
    for copy in copies:
        copy.start()
    for copy in copies:
        copy.wait()


def body(queries, key_vectors, values, out_proj, grad_out, windows, slab_order):
    hbm = pl.BlockSpec(memory_space=pltpu.HBM)
    smem = pl.BlockSpec(memory_space=pltpu.SMEM)
    vmem = pl.BlockSpec(memory_space=pltpu.VMEM)
    wide = RATIO * ROWS
    shapes = ((ROWS, 1024), (ROWS, RATIO * DIM), (ROWS, DIM), (ROWS, DIM))
    results = pl.pallas_call(
        kernel,
        name="layer",
        out_shape=tuple(pltpu.VMEM(shape, BF) for shape in shapes),
        in_specs=[smem, smem, hbm, hbm, hbm, hbm, hbm],
        out_specs=(vmem, vmem, vmem, vmem),
        scratch_shapes=[
            pltpu.VMEM((ROWS, RATIO * DIM), BF),
            pltpu.VMEM((10, 2, ROWS, DIM), BF),
            pltpu.VMEM((RATIO * DIM, 4096), BF),
            pltpu.VMEM((4, ROWS, 1024), BF),
            pltpu.VMEM((DIM, wide), BF),
            pltpu.VMEM((wide, DIM), BF),
            pltpu.VMEM((9, ROWS, wide), F32),
            pltpu.VMEM((1, wide), F32),
            pltpu.VMEM((1, wide), F32),
            pltpu.VMEM((DIM, wide), F32),
            pltpu.VMEM((ROWS, RATIO * DIM), F32),
            pltpu.VMEM((wide, DIM), BF),
            pltpu.VMEM((DIM, wide), BF),
            pltpu.VMEM((1, wide), F32),
            pltpu.VMEM((1, wide), F32),
            pltpu.VMEM((DIM, wide), F32),
            pltpu.VMEM((ROWS, RATIO * DIM), BF),
            pltpu.VMEM((2, ROWS, 1024), BF),
            pltpu.VMEM((ROWS, 1024), BF),
            pltpu.VMEM((2, ROWS, 1024), BF),
            pltpu.VMEM((ROWS, 1024), BF),
            pltpu.VMEM((8, 2, ROWS, DIM), BF),
            pltpu.VMEM((4, 2, 2, ROWS, DIM), BF),
            pltpu.VMEM((2, 2, ROWS, DIM), BF),
            pltpu.VMEM((2, 2, ROWS, DIM), BF),
            pltpu.VMEM((2, ROWS, DIM), BF),
            pltpu.VMEM((2, ROWS, DIM), BF),
            pltpu.VMEM((2, 2, 2, ROWS, DIM), F32),
            pltpu.VMEM((ROWS, ROWS), jnp.int32),
            pltpu.SemaphoreType.DMA((5,)),
            pltpu.SemaphoreType.DMA((9, 2)),
            pltpu.SemaphoreType.DMA((10, 2)),
            pltpu.SemaphoreType.DMA((5,)),
            pltpu.SemaphoreType.DMA((5,)),
            pltpu.SemaphoreType.DMA((3,)),
            pltpu.SemaphoreType.DMA((3,)),
            pltpu.SemaphoreType.DMA((8,)),
            pltpu.SemaphoreType.DMA((4, 2)),
            pltpu.SemaphoreType.DMA((2, 2)),
            pltpu.SemaphoreType.DMA((2, 2)),
            pltpu.SemaphoreType.DMA((2,)),
            pltpu.SemaphoreType.DMA((2,)),
        ],
        compiler_params=pltpu.CompilerParams(collective_id=0, has_side_effects=True, vmem_limit_bytes=56 * 1024 * 1024),
    )(slab_order, windows, queries, key_vectors, values, out_proj, grad_out)
    return pl.pallas_call(
        finish,
        name="finish",
        out_shape=tuple(jax.ShapeDtypeStruct(shape, BF) for shape in shapes),
        in_specs=[vmem] * 4,
        out_specs=(hbm,) * 4,
        scratch_shapes=[pltpu.SemaphoreType.DMA((4,))],
        compiler_params=pltpu.CompilerParams(vmem_limit_bytes=8 * 1024 * 1024),
    )(*results)


def solution(mesh):
    in_specs = (
        P("seq", "head"),
        P("seq", "head"),
        P("seq", "head"),
        P("head", None),
        P("seq", "head"),
        P("head"),
        P(),
    )
    out_specs = (P("seq", "head"), P("seq", "head"), P("seq", "head"), P("seq", "head"))
    return jax.shard_map(body, mesh=mesh, in_specs=in_specs, out_specs=out_specs, check_vma=False)
```

```python
import jax
import jax.numpy as jnp
from jax import lax
from jax.experimental import pallas as pl
from jax.experimental.pallas import tpu as pltpu
from jax.sharding import PartitionSpec as P

MESH = pl.DeviceIdType.MESH
BF = jnp.bfloat16
F32 = jnp.float32
ROWS = 256
DIM = 128
RATIO = 4
SCALE = DIM ** (-0.5)
LOG2E = 1.4426950408889634
LOWEST = -1e30
OWN, SPARE = 8, 9


def nn(a, b):
    return jnp.dot(a, b, preferred_element_type=F32)


def nt(a, b):
    return lax.dot_general(a, b, (((1,), (1,)), ((), ())), preferred_element_type=F32)


def kernel(
    order_hbm, spans_hbm, q_hbm, k_hbm, v_hbm, w_hbm, g_hbm,
    out_ref, gq_ref, gk_ref, gv_ref,
    qv, kv, w, gb, qt, qs, st, peak, total, acc, gsum, dos, dot_t, lse, delta, dqt, attn,
    sh_send, sh_f0, sh_part, sh_opp, dsend, drecv, ysend, yrecv, zsend, zrecv, dacc, place, whole, order, spans,
    lsem, c_send, c_recv, a_send, a_recv, b_send, b_recv, d_send, d_recv, y_send, y_recv, z_send, z_recv,
):
    s = lax.axis_index("seq")
    hd = lax.axis_index("head")
    y, x, zl = s // 8, (s // 2) % 4, s % 2
    zh, core = hd // 2, hd % 2
    r = 2 * x + zl
    rp = 2 * x + 1 - zl
    row0 = y * 8
    up = ((y + 1) % 4) * 8
    down = ((y + 3) % 4) * 8
    partner = {"head": 2 * zh + 1 - core}
    opposite = {"head": 2 * (1 - zh) + core}
    q0, q1 = 2 * zh + core, 2 * zh + 1 - core
    f0, f1 = 2 * (1 - zh) + core, 2 * (1 - zh) + 1 - core

    def at_seq(index):
        return {"seq": index}

    def remote(src, dst, send, recv, device):
        return pltpu.make_async_remote_copy(
            src_ref=src, dst_ref=dst, send_sem=send, recv_sem=recv, device_id=device, device_id_type=MESH
        )

    loads = [
        pltpu.make_async_copy(k_hbm, kv.at[OWN, 0], lsem.at[0]),
        pltpu.make_async_copy(v_hbm, kv.at[OWN, 1], lsem.at[1]),
        pltpu.make_async_copy(g_hbm, gb.at[0], lsem.at[2]),
        pltpu.make_async_copy(q_hbm, qv, lsem.at[3]),
        pltpu.make_async_copy(w_hbm, w, lsem.at[4]),
        pltpu.make_async_copy(order_hbm, order, lsem.at[5]),
        pltpu.make_async_copy(spans_hbm, spans, lsem.at[6]),
    ]
    for load in loads:
        load.start()

    barrier = pltpu.get_barrier_semaphore()
    for away in range(1, 4):
        pl.semaphore_signal(barrier, inc=1, device_id=at_seq(row0 + (r + 2 * away) % 8), device_id_type=MESH)
    for device in (at_seq(row0 + rp), partner, opposite, at_seq(up + r), at_seq(down + r)):
        pl.semaphore_signal(barrier, inc=1, device_id=device, device_id_type=MESH)
    edge = jnp.logical_or(x == 0, x == 3)

    @pl.when(edge)
    def _():
        corner = jnp.where(x == 3, up + zl, down + 6 + zl)
        pl.semaphore_signal(barrier, inc=1, device_id=at_seq(corner), device_id_type=MESH)

    pl.semaphore_wait(barrier, jnp.where(edge, 9, 8))

    op_slot = jnp.where(zl == 0, SPARE, r - 1)
    yp_slot = jnp.where(zl == 0, r + 1, SPARE)
    op_there = jnp.where(zl == 1, SPARE, r)

    def kv_copy(src, dst, part, send, device):
        return remote(kv.at[src, part], kv.at[dst, part], c_send.at[send, part], c_recv.at[dst, part], device)

    def side(away, other, part):
        xx = (x + away) % 4
        straight = jnp.logical_and(x == 3, away == 1)
        later = jnp.logical_or(xx > x, straight)
        row = jnp.where(straight, up, row0)
        if other:
            src = jnp.where(later, op_slot, yp_slot)
        else:
            src = jnp.where(later, OWN, r)
        dst = rp if other else r
        return later, kv_copy(src, dst, part, 3 + 2 * (away - 1) + other, at_seq(row + 2 * xx + zl))

    def start_sides(other, later_now, part):
        for away in (2, 1, 3):
            later, copy = side(away, other, part)

            @pl.when(later if later_now else jnp.logical_not(later))
            def _():
                copy.start()

    def own_copy(part, dst, send, device):
        return remote((k_hbm, v_hbm)[part], kv.at[dst, part], c_send.at[send, part], c_recv.at[dst, part], device)

    def to_half(part):
        return own_copy(part, op_there, 0, at_seq(row0 + rp))

    def to_up(part):
        return own_copy(part, r, 1, at_seq(up + r))

    def op_up(part):
        return kv_copy(op_slot, yp_slot, part, 2, at_seq(up + r))

    def await_part(slot, part):
        kv_copy(OWN, slot, part, 0, at_seq(row0 + rp)).wait_recv()

    for part in (0, 1):
        to_half(part).start()
        to_up(part).start()
    for part in (0, 1):
        loads[part].wait()
        start_sides(0, True, part)
    pieces = 4
    piece = ROWS // pieces
    a_opp = [
        remote(gb.at[0, pl.ds(i * piece, piece)], gb.at[2, pl.ds(i * piece, piece)], a_send.at[i], a_recv.at[i], opposite)
        for i in range(pieces)
    ]
    a_part = remote(gb.at[0], gb.at[1], a_send.at[2 * pieces], a_recv.at[2 * pieces], partner)
    a_fwd = [
        remote(gb.at[2, pl.ds(i * piece, piece)], gb.at[3, pl.ds(i * piece, piece)], a_send.at[pieces + i], a_recv.at[pieces + i], partner)
        for i in range(pieces)
    ]
    place[...] = lax.broadcasted_iota(jnp.int32, (ROWS, ROWS), 1) - lax.broadcasted_iota(jnp.int32, (ROWS, ROWS), 0)
    dqt[...] = jnp.zeros_like(dqt)
    dacc[zl, 1] = jnp.zeros((2, ROWS, DIM), F32)
    loads[3].wait()
    for h in range(RATIO):
        block = qv[:, h * DIM : (h + 1) * DIM]
        qs[pl.ds(h * ROWS, ROWS), :] = block
        qt[:, h * ROWS : (h + 1) * ROWS] = block.T
    loads[5].wait()
    loads[6].wait()
    mine = order[s]

    def forward(slot, hidden, first=False):
        key = kv[slot, 0]
        value_t = kv[slot, 1].T
        tops = []
        for h in range(RATIO):
            cols = slice(h * ROWS, (h + 1) * ROWS)
            scores = jnp.where(hidden(h), LOWEST, nn(key, qt[:, cols]) * (SCALE * LOG2E))
            st[slot, :, cols] = scores
            tops.append(jnp.max(scores, axis=0, keepdims=True))
        for h in range(RATIO):
            cols = slice(h * ROWS, (h + 1) * ROWS)
            if first:
                top = tops[h]
                probs = jnp.exp2(st[slot, :, cols] - top)
                total[:, cols] = jnp.sum(probs, axis=0, keepdims=True)
                acc[:, cols] = nn(value_t, probs.astype(BF))
            else:
                before = peak[:, cols]
                top = jnp.maximum(before, tops[h])
                fade = jnp.exp2(before - top)
                probs = jnp.exp2(st[slot, :, cols] - top)
                total[:, cols] = total[:, cols] * fade + jnp.sum(probs, axis=0, keepdims=True)
                acc[:, cols] = acc[:, cols] * fade + nn(value_t, probs.astype(BF))
            peak[:, cols] = top

    def forward_on(slot):
        row = jnp.where(slot < r, row0, down)
        gap = (mine - order[row + slot]) * ROWS

        def windowed(h):
            limit = jnp.where(gap > 0, spans[h] - gap, -100000)
            return place[...] >= limit

        forward(slot, windowed)

    def pair_slot(away, other):
        return 2 * ((x + away) % 4) + (zl + other) % 2

    forward(OWN, lambda h: place[...] < 0, first=True)

    loads[2].wait()
    a_part.start()
    for copy in a_opp:
        copy.start()

    for part in (0, 1):
        await_part(op_slot, part)
        op_up(part).start()
        start_sides(1, True, part)
    def row_before(slot, other, passing):
        @pl.when(x > 0 if passing else x == 0)
        def _():
            for part in (0, 1):
                await_part(slot, part)
                if passing:
                    start_sides(other, False, part)

    row_before(r, 0, True)

    loads[4].wait()

    def w_cols(quarter):
        return pl.ds(pl.multiple_of(quarter * 1024, 1024), 1024)

    gsum[...] = nt(gb[0], w[:, w_cols(q0)])
    a_part.wait_recv()
    gsum[...] += nt(gb[1], w[:, w_cols(q1)])

    def far_columns(group):
        rows = pl.ds(group * 128, 128)
        gsum[rows, :] += nt(gb[2, rows, :], w[:, w_cols(f0)])
        for i in (2 * group, 2 * group + 1):
            a_fwd[i].wait_recv()
        gsum[rows, :] += nt(gb[3, rows, :], w[:, w_cols(f1)])
        for h in range(RATIO):
            grad = gsum[rows, h * DIM : (h + 1) * DIM].astype(BF)
            dos[pl.ds(h * ROWS + group * 128, 128), :] = grad
            dot_t[:, pl.ds(h * ROWS + group * 128, 128)] = grad.T

    row_before(yp_slot, 1, True)

    def forward_step(j, carry):
        away = 3 - 2 * (j % 3) + 3 * ((j % 3) // 2)
        slot = pair_slot(away, j // 3)
        for part in (0, 1):
            await_part(slot, part)
        forward_on(slot)
        return carry

    def pass_on(*which):
        for i in which:
            a_opp[i].wait_recv()
            a_fwd[i].start()

    lax.fori_loop(0, 1, forward_step, 0)
    pass_on(0)
    lax.fori_loop(1, 2, forward_step, 0)
    row_before(r, 0, False)
    forward_on(r)
    pass_on(1)
    lax.fori_loop(2, 3, forward_step, 0)
    row_before(yp_slot, 1, False)
    forward_on(rp)
    lax.fori_loop(3, 4, forward_step, 0)
    pass_on(2)
    lax.fori_loop(4, 5, forward_step, 0)
    far_columns(0)
    lax.fori_loop(5, 6, forward_step, 0)

    norm = 1.0 / total[...]
    lse[...] = peak[...] + jnp.log(total[...]) * LOG2E
    for h in range(RATIO):
        cols = slice(h * ROWS, (h + 1) * ROWS)
        mixed = (acc[:, cols] * norm[:, cols]).astype(BF)
        attn[:, h * DIM : (h + 1) * DIM] = mixed.T
        acc[:, cols] = mixed.astype(F32)

    def share(quarter, i):
        return nn(attn[...], w[:, pl.ds(pl.multiple_of(quarter * 1024 + i * 512, 512), 512)])

    def b_part(which, i):
        return remote(sh_send.at[which, i], sh_part.at[which, i], b_send.at[which, i], b_recv.at[which, i], partner)

    def b_opp(i):
        return remote(sh_f0.at[i], sh_opp.at[i], b_send.at[2, i], b_recv.at[2, i], opposite)

    def share_out(i):
        b_part(0, i).wait_recv()
        sh_f0[i] = (share(f0, i) + sh_part[0, i].astype(F32)).astype(BF)
        b_opp(i).start()

    pass_on(3)
    for i in range(2):
        sh_send[0, i] = share(f1, i).astype(BF)
        b_part(0, i).start()
    far_columns(1)
    delta[...] = jnp.sum(dot_t[...].astype(F32) * acc[...], axis=0, keepdims=True)

    def backward(slot):
        key_t = kv[slot, 0].T
        value = kv[slot, 1]
        probs_all = []
        grads_all = []
        for h in range(RATIO):
            cols = slice(h * ROWS, (h + 1) * ROWS)
            probs = jnp.exp2(st[slot, :, cols] - lse[:, cols])
            grad_probs = nn(value, dot_t[:, cols])
            probs_all.append(probs.astype(BF))
            grads_all.append((probs * (grad_probs - delta[:, cols])).astype(BF))
        probs_all = jnp.concatenate(probs_all, axis=1)
        grads_all = jnp.concatenate(grads_all, axis=1)
        grad_key = nn(grads_all, qs[...]) * SCALE
        grad_value = nn(probs_all, dos[...])
        dqt[...] += nn(key_t, grads_all)
        return grad_key, grad_value

    def pair_grads(away, other):
        slot = pair_slot(away, other)
        return remote(
            dsend.at[slot], drecv.at[x, other], d_send.at[slot], d_recv.at[x, other], at_seq(row0 + 2 * ((x + away) % 4) + zl)
        )

    def backward_step(j, carry):
        turn, other = j % 3, 1 - j // 3
        away = jnp.where(x == 0, 3 - turn, 2 - turn + 3 * (turn // 2))
        slot = pair_slot(away, other)
        grad_key, grad_value = backward(slot)
        dsend[slot, 0] = grad_key.astype(BF)
        dsend[slot, 1] = grad_value.astype(BF)
        pair_grads(away, other).start()
        return carry

    lax.fori_loop(0, 1, backward_step, 0)
    share_out(0)
    lax.fori_loop(1, 2, backward_step, 0)
    share_out(1)
    lax.fori_loop(2, 6, backward_step, 0)

    def backward_here(slot, row, other):
        grad_key, grad_value = backward(slot)
        dacc[row, other, 0] = grad_key
        dacc[row, other, 1] = grad_value

    backward_here(rp, 1 - zl, 1)
    backward_here(r, 1, 0)

    def pair_from(index, other):
        return remote(dsend.at[r], drecv.at[index, other], d_send.at[r], d_recv.at[index, other], at_seq(row0 + rp))

    def y_copy(other, part):
        return remote(
            ysend.at[other, part], yrecv.at[other, part], y_send.at[other, part], y_recv.at[other, part], at_seq(down + r)
        )

    def z_copy(part):
        return remote(zsend.at[part], zrecv.at[part], z_send.at[part], z_recv.at[part], at_seq(row0 + rp))

    def add_from(index, row, other):
        pair_from(index, other).wait_recv()
        dacc[row, other] += drecv[index, other].astype(F32)

    def send_up(other):
        @pl.loop(0, x)
        def _(index):
            add_from(x - 1 - index, 1, other)

        for part in (0, 1):
            ysend[other, part] = dacc[1, other, part].astype(BF)
            y_copy(other, part).start()

    has_other = x + 1 - zl > 0
    backward_here(OWN, 0, 0)
    for i in range(2):
        sh_send[1, i] = share(q1, i).astype(BF)
        b_part(1, i).start()
    for h in range(RATIO):
        gq_ref[:, h * DIM : (h + 1) * DIM] = (dqt[:, h * ROWS : (h + 1) * ROWS] * SCALE).astype(BF).T
    for i in range(2):
        whole[i] = share(q0, i)
    @pl.when(has_other)
    def _():
        send_up(1)

    send_up(0)

    @pl.loop(x + 1, 4)
    def _(index):
        add_from(index, 0, 1)
        add_from(index, 0, 0)

    for part in (0, 1):

        @pl.when(has_other)
        def _():
            y_copy(1, part).wait_recv()
            zsend[part] = (dacc[0, 1, part] + yrecv[1, part].astype(F32)).astype(BF)

        @pl.when(jnp.logical_not(has_other))
        def _():
            zsend[part] = dacc[0, 1, part].astype(BF)

        z_copy(part).start()

    for i in range(2):
        b_part(1, i).wait_recv()
        b_opp(i).wait_recv()
        out_ref[:, i * 512 : (i + 1) * 512] = (whole[i] + sh_part[1, i].astype(F32) + sh_opp[i].astype(F32)).astype(BF)

    for part, result in ((0, gk_ref), (1, gv_ref)):
        y_copy(0, part).wait_recv()
        z_copy(part).wait_recv()
        result[...] = (dacc[0, 0, part] + yrecv[0, part].astype(F32) + zrecv[part].astype(F32)).astype(BF)

    for part in (0, 1):
        for copy in (to_half(part), to_up(part), op_up(part), y_copy(0, part), z_copy(part)):
            copy.wait_send()
        for away in (1, 2, 3):
            for other in (0, 1):
                side(away, other, part)[1].wait_send()

        @pl.when(has_other)
        def _():
            y_copy(1, part).wait_send()

    for copy in (a_part, *a_opp, *a_fwd, *(b_part(n, i) for n in range(2) for i in range(2)), b_opp(0), b_opp(1)):
        copy.wait_send()
    for away in (1, 2, 3):
        for other in (0, 1):
            pair_grads(away, other).wait_send()


def finish(*refs):
    ins, outs, sems = refs[:4], refs[4:8], refs[8]
    copies = [pltpu.make_async_copy(a, b, sems.at[i]) for i, (a, b) in enumerate(zip(ins, outs))]
    for copy in copies:
        copy.start()
    for copy in copies:
        copy.wait()


def body(queries, key_vectors, values, out_proj, grad_out, windows, slab_order):
    hbm = pl.BlockSpec(memory_space=pltpu.HBM)
    vmem = pl.BlockSpec(memory_space=pltpu.VMEM)
    wide = RATIO * ROWS
    shapes = ((ROWS, 1024), (ROWS, RATIO * DIM), (ROWS, DIM), (ROWS, DIM))
    results = pl.pallas_call(
        kernel,
        name="layer",
        out_shape=tuple(pltpu.VMEM(shape, BF) for shape in shapes),
        in_specs=[hbm] * 7,
        out_specs=(vmem, vmem, vmem, vmem),
        scratch_shapes=[
            pltpu.VMEM((ROWS, RATIO * DIM), BF),
            pltpu.VMEM((10, 2, ROWS, DIM), BF),
            pltpu.VMEM((RATIO * DIM, 4096), BF),
            pltpu.VMEM((4, ROWS, 1024), BF),
            pltpu.VMEM((DIM, wide), BF),
            pltpu.VMEM((wide, DIM), BF),
            pltpu.VMEM((9, ROWS, wide), F32),
            pltpu.VMEM((1, wide), F32),
            pltpu.VMEM((1, wide), F32),
            pltpu.VMEM((DIM, wide), F32),
            pltpu.VMEM((ROWS, RATIO * DIM), F32),
            pltpu.VMEM((wide, DIM), BF),
            pltpu.VMEM((DIM, wide), BF),
            pltpu.VMEM((1, wide), F32),
            pltpu.VMEM((1, wide), F32),
            pltpu.VMEM((DIM, wide), F32),
            pltpu.VMEM((ROWS, RATIO * DIM), BF),
            pltpu.VMEM((2, 2, ROWS, 512), BF),
            pltpu.VMEM((2, ROWS, 512), BF),
            pltpu.VMEM((2, 2, ROWS, 512), BF),
            pltpu.VMEM((2, ROWS, 512), BF),
            pltpu.VMEM((8, 2, ROWS, DIM), BF),
            pltpu.VMEM((4, 2, 2, ROWS, DIM), BF),
            pltpu.VMEM((2, 2, ROWS, DIM), BF),
            pltpu.VMEM((2, 2, ROWS, DIM), BF),
            pltpu.VMEM((2, ROWS, DIM), BF),
            pltpu.VMEM((2, ROWS, DIM), BF),
            pltpu.VMEM((2, 2, 2, ROWS, DIM), F32),
            pltpu.VMEM((ROWS, ROWS), jnp.int32),
            pltpu.VMEM((2, ROWS, 512), F32),
            pltpu.SMEM((32,), jnp.int32),
            pltpu.SMEM((RATIO,), jnp.int32),
            pltpu.SemaphoreType.DMA((7,)),
            pltpu.SemaphoreType.DMA((9, 2)),
            pltpu.SemaphoreType.DMA((10, 2)),
            pltpu.SemaphoreType.DMA((9,)),
            pltpu.SemaphoreType.DMA((9,)),
            pltpu.SemaphoreType.DMA((3, 2)),
            pltpu.SemaphoreType.DMA((3, 2)),
            pltpu.SemaphoreType.DMA((8,)),
            pltpu.SemaphoreType.DMA((4, 2)),
            pltpu.SemaphoreType.DMA((2, 2)),
            pltpu.SemaphoreType.DMA((2, 2)),
            pltpu.SemaphoreType.DMA((2,)),
            pltpu.SemaphoreType.DMA((2,)),
        ],
        compiler_params=pltpu.CompilerParams(collective_id=0, has_side_effects=True, vmem_limit_bytes=56 * 1024 * 1024),
    )(slab_order, windows, queries, key_vectors, values, out_proj, grad_out)
    return pl.pallas_call(
        finish,
        name="finish",
        out_shape=tuple(jax.ShapeDtypeStruct(shape, BF) for shape in shapes),
        in_specs=[vmem] * 4,
        out_specs=(hbm,) * 4,
        scratch_shapes=[pltpu.SemaphoreType.DMA((4,))],
        compiler_params=pltpu.CompilerParams(vmem_limit_bytes=8 * 1024 * 1024),
    )(*results)


def solution(mesh):
    in_specs = (
        P("seq", "head"),
        P("seq", "head"),
        P("seq", "head"),
        P("head", None),
        P("seq", "head"),
        P("head"),
        P(),
    )
    out_specs = (P("seq", "head"), P("seq", "head"), P("seq", "head"), P("seq", "head"))
    return jax.shard_map(body, mesh=mesh, in_specs=in_specs, out_specs=out_specs, check_vma=False)
```

```python
import jax
import jax.numpy as jnp
from jax import lax
from jax.experimental import pallas as pl
from jax.experimental.pallas import tpu as pltpu
from jax.sharding import PartitionSpec as P

MESH = pl.DeviceIdType.MESH
BF = jnp.bfloat16
F32 = jnp.float32
ROWS = 256
DIM = 128
RATIO = 4
SCALE = DIM ** (-0.5)
LOG2E = 1.4426950408889634
LOWEST = -1e30
OWN, SPARE = 8, 9


def nn(a, b):
    return jnp.dot(a, b, preferred_element_type=F32)


def nt(a, b):
    return lax.dot_general(a, b, (((1,), (1,)), ((), ())), preferred_element_type=F32)


def kernel(
    order_hbm, spans_hbm, q_hbm, k_hbm, v_hbm, w_hbm, g_hbm,
    out_ref, gq_ref, gk_ref, gv_ref,
    qv, kv, w, gb, qt, qs, st, peak, total, acc, gsum, dos, dot_t, lse, delta, dqt, attn,
    sh_send, sh_f0, sh_part, sh_opp, dsend, drecv, ysend, yrecv, zsend, zrecv, dacc, place, whole, order, spans,
    lsem, c_send, c_recv, a_send, a_recv, b_send, b_recv, d_send, d_recv, y_send, y_recv, z_send, z_recv,
):
    s = lax.axis_index("seq")
    hd = lax.axis_index("head")
    y, x, zl = s // 8, (s // 2) % 4, s % 2
    zh, core = hd // 2, hd % 2
    r = 2 * x + zl
    rp = 2 * x + 1 - zl
    row0 = y * 8
    up = ((y + 1) % 4) * 8
    down = ((y + 3) % 4) * 8
    partner = {"head": 2 * zh + 1 - core}
    opposite = {"head": 2 * (1 - zh) + core}
    q0, q1 = 2 * zh + core, 2 * zh + 1 - core
    f0, f1 = 2 * (1 - zh) + core, 2 * (1 - zh) + 1 - core

    def at_seq(index):
        return {"seq": index}

    def remote(src, dst, send, recv, device):
        return pltpu.make_async_remote_copy(
            src_ref=src, dst_ref=dst, send_sem=send, recv_sem=recv, device_id=device, device_id_type=MESH
        )

    loads = [
        pltpu.make_async_copy(k_hbm, kv.at[OWN, 0], lsem.at[0]),
        pltpu.make_async_copy(v_hbm, kv.at[OWN, 1], lsem.at[1]),
        pltpu.make_async_copy(g_hbm, gb.at[0], lsem.at[2]),
        pltpu.make_async_copy(q_hbm, qv, lsem.at[3]),
        pltpu.make_async_copy(w_hbm, w, lsem.at[4]),
        pltpu.make_async_copy(order_hbm, order, lsem.at[5]),
        pltpu.make_async_copy(spans_hbm, spans, lsem.at[6]),
    ]
    for load in loads:
        load.start()

    barrier = pltpu.get_barrier_semaphore()
    for away in range(1, 4):
        pl.semaphore_signal(barrier, inc=1, device_id=at_seq(row0 + (r + 2 * away) % 8), device_id_type=MESH)
    for device in (at_seq(row0 + rp), partner, opposite, at_seq(up + r), at_seq(down + r)):
        pl.semaphore_signal(barrier, inc=1, device_id=device, device_id_type=MESH)
    edge = jnp.logical_or(x == 0, x == 3)

    @pl.when(edge)
    def _():
        corner = jnp.where(x == 3, up + zl, down + 6 + zl)
        pl.semaphore_signal(barrier, inc=1, device_id=at_seq(corner), device_id_type=MESH)

    pl.semaphore_wait(barrier, jnp.where(edge, 9, 8))

    op_slot = jnp.where(zl == 0, SPARE, r - 1)
    yp_slot = jnp.where(zl == 0, r + 1, SPARE)
    op_there = jnp.where(zl == 1, SPARE, r)

    def kv_copy(src, dst, part, send, device):
        return remote(kv.at[src, part], kv.at[dst, part], c_send.at[send, part], c_recv.at[dst, part], device)

    def side(away, other, part):
        xx = (x + away) % 4
        straight = jnp.logical_and(x == 3, away == 1)
        later = jnp.logical_or(xx > x, straight)
        row = jnp.where(straight, up, row0)
        if other:
            src = jnp.where(later, op_slot, yp_slot)
        else:
            src = jnp.where(later, OWN, r)
        dst = rp if other else r
        return later, kv_copy(src, dst, part, 3 + 2 * (away - 1) + other, at_seq(row + 2 * xx + zl))

    def start_sides(other, later_now, part):
        for away in (2, 1, 3):
            later, copy = side(away, other, part)

            @pl.when(later if later_now else jnp.logical_not(later))
            def _():
                copy.start()

    def own_copy(part, dst, send, device):
        return remote((k_hbm, v_hbm)[part], kv.at[dst, part], c_send.at[send, part], c_recv.at[dst, part], device)

    def to_half(part):
        return own_copy(part, op_there, 0, at_seq(row0 + rp))

    def to_up(part):
        return own_copy(part, r, 1, at_seq(up + r))

    def op_up(part):
        return kv_copy(op_slot, yp_slot, part, 2, at_seq(up + r))

    def await_part(slot, part):
        kv_copy(OWN, slot, part, 0, at_seq(row0 + rp)).wait_recv()

    for part in (0, 1):
        to_half(part).start()
        to_up(part).start()
    for part in (0, 1):
        loads[part].wait()
        start_sides(0, True, part)
    pieces = 4
    piece = ROWS // pieces
    a_opp = [
        remote(gb.at[0, pl.ds(i * piece, piece)], gb.at[2, pl.ds(i * piece, piece)], a_send.at[i], a_recv.at[i], opposite)
        for i in range(pieces)
    ]
    a_part = remote(gb.at[0], gb.at[1], a_send.at[2 * pieces], a_recv.at[2 * pieces], partner)
    a_fwd = [
        remote(gb.at[2, pl.ds(i * piece, piece)], gb.at[3, pl.ds(i * piece, piece)], a_send.at[pieces + i], a_recv.at[pieces + i], partner)
        for i in range(pieces)
    ]
    place[...] = lax.broadcasted_iota(jnp.int32, (ROWS, ROWS), 1) - lax.broadcasted_iota(jnp.int32, (ROWS, ROWS), 0)
    dqt[...] = jnp.zeros_like(dqt)
    dacc[zl, 1] = jnp.zeros((2, ROWS, DIM), F32)
    loads[3].wait()
    for h in range(RATIO):
        block = qv[:, h * DIM : (h + 1) * DIM]
        qs[pl.ds(h * ROWS, ROWS), :] = block
        qt[:, h * ROWS : (h + 1) * ROWS] = block.T
    loads[5].wait()
    loads[6].wait()
    mine = order[s]

    def forward(slot, hidden, first=False):
        key = kv[slot, 0]
        value_t = kv[slot, 1].T
        tops = []
        for h in range(RATIO):
            cols = slice(h * ROWS, (h + 1) * ROWS)
            scores = jnp.where(hidden(h), LOWEST, nn(key, qt[:, cols]) * (SCALE * LOG2E))
            st[slot, :, cols] = scores
            tops.append(jnp.max(scores, axis=0, keepdims=True))
        for h in range(RATIO):
            cols = slice(h * ROWS, (h + 1) * ROWS)
            if first:
                top = tops[h]
                probs = jnp.exp2(st[slot, :, cols] - top)
                total[:, cols] = jnp.sum(probs, axis=0, keepdims=True)
                acc[:, cols] = nn(value_t, probs.astype(BF))
            else:
                before = peak[:, cols]
                top = jnp.maximum(before, tops[h])
                fade = jnp.exp2(before - top)
                probs = jnp.exp2(st[slot, :, cols] - top)
                total[:, cols] = total[:, cols] * fade + jnp.sum(probs, axis=0, keepdims=True)
                acc[:, cols] = acc[:, cols] * fade + nn(value_t, probs.astype(BF))
            peak[:, cols] = top

    def forward_on(slot):
        row = jnp.where(slot < r, row0, down)
        gap = (mine - order[row + slot]) * ROWS

        def windowed(h):
            limit = jnp.where(gap > 0, spans[h] - gap, -100000)
            return place[...] >= limit

        forward(slot, windowed)

    def pair_slot(away, other):
        return 2 * ((x + away) % 4) + (zl + other) % 2

    forward(OWN, lambda h: place[...] < 0, first=True)

    loads[2].wait()
    a_part.start()
    for copy in a_opp:
        copy.start()

    for part in (0, 1):
        await_part(op_slot, part)
        op_up(part).start()
        start_sides(1, True, part)
    def row_before(slot, other, passing):
        @pl.when(x > 0 if passing else x == 0)
        def _():
            for part in (0, 1):
                await_part(slot, part)
                if passing:
                    start_sides(other, False, part)

    row_before(r, 0, True)

    loads[4].wait()

    def w_cols(quarter):
        return pl.ds(pl.multiple_of(quarter * 1024, 1024), 1024)

    gsum[...] = nt(gb[0], w[:, w_cols(q0)])
    a_part.wait_recv()
    gsum[...] += nt(gb[1], w[:, w_cols(q1)])

    def far_columns(group):
        rows = pl.ds(group * 128, 128)
        gsum[rows, :] += nt(gb[2, rows, :], w[:, w_cols(f0)])
        for i in (2 * group, 2 * group + 1):
            a_fwd[i].wait_recv()
        gsum[rows, :] += nt(gb[3, rows, :], w[:, w_cols(f1)])
        for h in range(RATIO):
            grad = gsum[rows, h * DIM : (h + 1) * DIM].astype(BF)
            dos[pl.ds(h * ROWS + group * 128, 128), :] = grad
            dot_t[:, pl.ds(h * ROWS + group * 128, 128)] = grad.T

    row_before(yp_slot, 1, True)

    def pass_on(*which):
        for i in which:
            a_opp[i].wait_recv()
            a_fwd[i].start()

    orders = (
        ((3, 0), (1, 0), 0, (2, 0), 1, (3, 1), (1, 1), (2, 1)),
        (0, 1, (3, 0), (3, 1), (1, 0), (2, 0), (1, 1), (2, 1)),
        (0, 1, (3, 0), (2, 0), (3, 1), (2, 1), (1, 0), (1, 1)),
        (0, 1, (3, 0), (2, 0), (1, 0), (3, 1), (2, 1), (1, 1)),
    )

    def by_x(values):
        return jnp.where(x == 0, values[0], jnp.where(x == 1, values[1], jnp.where(x == 2, values[2], values[3])))

    def slot_of(what):
        if what == 0:
            return r
        return rp if what == 1 else pair_slot(*what)

    def forward_step(i):
        picks = [order_x[i] for order_x in orders]
        slot = by_x([slot_of(what) for what in picks])
        paired = by_x([int(isinstance(what, tuple)) for what in picks])

        @pl.when(paired == 1)
        def _():
            for part in (0, 1):
                await_part(slot, part)

        if i == 2:
            row_before(r, 0, False)
        if i == 4:
            row_before(yp_slot, 1, False)
        forward_on(slot)

    for i in range(3):
        forward_step(i)
    pass_on(0)
    forward_step(3)
    pass_on(1)
    forward_step(4)
    forward_step(5)
    pass_on(2)
    forward_step(6)
    forward_step(7)

    norm = 1.0 / total[...]
    lse[...] = peak[...] + jnp.log(total[...]) * LOG2E
    for h in range(RATIO):
        cols = slice(h * ROWS, (h + 1) * ROWS)
        mixed = (acc[:, cols] * norm[:, cols]).astype(BF)
        attn[:, h * DIM : (h + 1) * DIM] = mixed.T
        acc[:, cols] = mixed.astype(F32)

    def share(quarter, i):
        return nn(attn[...], w[:, pl.ds(pl.multiple_of(quarter * 1024 + i * 512, 512), 512)])

    def b_part(which, i):
        return remote(sh_send.at[which, i], sh_part.at[which, i], b_send.at[which, i], b_recv.at[which, i], partner)

    def b_opp(i):
        return remote(sh_f0.at[i], sh_opp.at[i], b_send.at[2, i], b_recv.at[2, i], opposite)

    def share_out(i):
        b_part(0, i).wait_recv()
        sh_f0[i] = (share(f0, i) + sh_part[0, i].astype(F32)).astype(BF)
        b_opp(i).start()

    pass_on(3)
    for i in range(2):
        sh_send[0, i] = share(f1, i).astype(BF)
        b_part(0, i).start()
    far_columns(0)
    far_columns(1)
    delta[...] = jnp.sum(dot_t[...].astype(F32) * acc[...], axis=0, keepdims=True)

    def backward(slot):
        key_t = kv[slot, 0].T
        value = kv[slot, 1]
        probs_all = []
        grads_all = []
        for h in range(RATIO):
            cols = slice(h * ROWS, (h + 1) * ROWS)
            probs = jnp.exp2(st[slot, :, cols] - lse[:, cols])
            grad_probs = nn(value, dot_t[:, cols])
            probs_all.append(probs.astype(BF))
            grads_all.append((probs * (grad_probs - delta[:, cols])).astype(BF))
        probs_all = jnp.concatenate(probs_all, axis=1)
        grads_all = jnp.concatenate(grads_all, axis=1)
        grad_key = nn(grads_all, qs[...]) * SCALE
        grad_value = nn(probs_all, dos[...])
        dqt[...] += nn(key_t, grads_all)
        return grad_key, grad_value

    def pair_grads(away, other, part):
        slot = pair_slot(away, other)
        return remote(
            dsend.at[slot, part],
            drecv.at[x, other, part],
            d_send.at[slot, part],
            d_recv.at[x, other, part],
            at_seq(row0 + 2 * ((x + away) % 4) + zl),
        )

    def turn_away(turn):
        return jnp.where(x == 0, 3 - turn, 2 - turn + 3 * (turn // 2))

    def backward_step(j, carry):
        other = 1 - j // 3
        away = turn_away(j % 3)
        slot = pair_slot(away, other)
        grad_key, grad_value = backward(slot)
        dsend[slot, 0] = grad_key.astype(BF)
        pair_grads(away, other, 0).start()
        dsend[slot, 1] = grad_value.astype(BF)

        @pl.when(other == 1)
        def _():
            pair_grads(away, other, 1).start()

        return carry

    share_out(0)
    lax.fori_loop(0, 2, backward_step, 0)
    share_out(1)
    lax.fori_loop(2, 6, backward_step, 0)
    for turn in range(3):
        pair_grads(turn_away(turn), 0, 1).start()

    def backward_here(slot, row, other):
        grad_key, grad_value = backward(slot)
        dacc[row, other, 0] = grad_key
        dacc[row, other, 1] = grad_value

    backward_here(rp, 1 - zl, 1)
    backward_here(r, 1, 0)

    def pair_from(index, other, part):
        return remote(
            dsend.at[r, part], drecv.at[index, other, part], d_send.at[r, part], d_recv.at[index, other, part], at_seq(row0 + rp)
        )

    def y_copy(other, part):
        return remote(
            ysend.at[other, part], yrecv.at[other, part], y_send.at[other, part], y_recv.at[other, part], at_seq(down + r)
        )

    def z_copy(part):
        return remote(zsend.at[part], zrecv.at[part], z_send.at[part], z_recv.at[part], at_seq(row0 + rp))

    def add_from(index, row, other, part):
        pair_from(index, other, part).wait_recv()
        dacc[row, other, part] += drecv[index, other, part].astype(F32)

    def send_up(other, part):
        @pl.loop(0, x)
        def _(index):
            add_from(x - 1 - index, 1, other, part)

        ysend[other, part] = dacc[1, other, part].astype(BF)
        y_copy(other, part).start()

    def add_later(other, part):
        @pl.loop(x + 1, 4)
        def _(index):
            add_from(index, 0, other, part)

    has_other = x + 1 - zl > 0
    backward_here(OWN, 0, 0)
    for i in range(2):
        sh_send[1, i] = share(q1, i).astype(BF)
        b_part(1, i).start()
    for h in range(RATIO):
        gq_ref[:, h * DIM : (h + 1) * DIM] = (dqt[:, h * ROWS : (h + 1) * ROWS] * SCALE).astype(BF).T
    for i in range(2):
        whole[i] = share(q0, i)
    @pl.when(has_other)
    def _():
        for part in (0, 1):
            send_up(1, part)

    for part in (0, 1):
        add_later(1, part)
    send_up(0, 0)
    add_later(0, 0)

    for part in (0, 1):

        @pl.when(has_other)
        def _():
            y_copy(1, part).wait_recv()
            zsend[part] = (dacc[0, 1, part] + yrecv[1, part].astype(F32)).astype(BF)

        @pl.when(jnp.logical_not(has_other))
        def _():
            zsend[part] = dacc[0, 1, part].astype(BF)

        z_copy(part).start()

    send_up(0, 1)
    add_later(0, 1)

    for i in range(2):
        b_part(1, i).wait_recv()
        b_opp(i).wait_recv()
        out_ref[:, i * 512 : (i + 1) * 512] = (whole[i] + sh_part[1, i].astype(F32) + sh_opp[i].astype(F32)).astype(BF)

    for part in (0, 1):
        for copy in (to_half(part), to_up(part), op_up(part)):
            copy.wait_send()
        for away in (1, 2, 3):
            for other in (0, 1):
                side(away, other, part)[1].wait_send()

        @pl.when(has_other)
        def _():
            y_copy(1, part).wait_send()

    for copy in (a_part, *a_opp, *a_fwd, *(b_part(n, i) for n in range(2) for i in range(2)), b_opp(0), b_opp(1)):
        copy.wait_send()
    for away in (1, 2, 3):
        for other in (0, 1):
            for part in (0, 1):
                pair_grads(away, other, part).wait_send()
    for part in (0, 1):
        y_copy(0, part).wait_send()
        z_copy(part).wait_send()

    for part, result in ((0, gk_ref), (1, gv_ref)):
        y_copy(0, part).wait_recv()
        z_copy(part).wait_recv()
        result[...] = (dacc[0, 0, part] + yrecv[0, part].astype(F32) + zrecv[part].astype(F32)).astype(BF)


def finish(*refs):
    ins, outs, sems = refs[:4], refs[4:8], refs[8]
    copies = [pltpu.make_async_copy(a, b, sems.at[i]) for i, (a, b) in enumerate(zip(ins, outs))]
    for copy in copies:
        copy.start()
    for copy in copies:
        copy.wait()


def body(queries, key_vectors, values, out_proj, grad_out, windows, slab_order):
    hbm = pl.BlockSpec(memory_space=pltpu.HBM)
    vmem = pl.BlockSpec(memory_space=pltpu.VMEM)
    wide = RATIO * ROWS
    shapes = ((ROWS, 1024), (ROWS, RATIO * DIM), (ROWS, DIM), (ROWS, DIM))
    results = pl.pallas_call(
        kernel,
        name="layer",
        out_shape=tuple(pltpu.VMEM(shape, BF) for shape in shapes),
        in_specs=[hbm] * 7,
        out_specs=(vmem, vmem, vmem, vmem),
        scratch_shapes=[
            pltpu.VMEM((ROWS, RATIO * DIM), BF),
            pltpu.VMEM((10, 2, ROWS, DIM), BF),
            pltpu.VMEM((RATIO * DIM, 4096), BF),
            pltpu.VMEM((4, ROWS, 1024), BF),
            pltpu.VMEM((DIM, wide), BF),
            pltpu.VMEM((wide, DIM), BF),
            pltpu.VMEM((9, ROWS, wide), F32),
            pltpu.VMEM((1, wide), F32),
            pltpu.VMEM((1, wide), F32),
            pltpu.VMEM((DIM, wide), F32),
            pltpu.VMEM((ROWS, RATIO * DIM), F32),
            pltpu.VMEM((wide, DIM), BF),
            pltpu.VMEM((DIM, wide), BF),
            pltpu.VMEM((1, wide), F32),
            pltpu.VMEM((1, wide), F32),
            pltpu.VMEM((DIM, wide), F32),
            pltpu.VMEM((ROWS, RATIO * DIM), BF),
            pltpu.VMEM((2, 2, ROWS, 512), BF),
            pltpu.VMEM((2, ROWS, 512), BF),
            pltpu.VMEM((2, 2, ROWS, 512), BF),
            pltpu.VMEM((2, ROWS, 512), BF),
            pltpu.VMEM((8, 2, ROWS, DIM), BF),
            pltpu.VMEM((4, 2, 2, ROWS, DIM), BF),
            pltpu.VMEM((2, 2, ROWS, DIM), BF),
            pltpu.VMEM((2, 2, ROWS, DIM), BF),
            pltpu.VMEM((2, ROWS, DIM), BF),
            pltpu.VMEM((2, ROWS, DIM), BF),
            pltpu.VMEM((2, 2, 2, ROWS, DIM), F32),
            pltpu.VMEM((ROWS, ROWS), jnp.int32),
            pltpu.VMEM((2, ROWS, 512), F32),
            pltpu.SMEM((32,), jnp.int32),
            pltpu.SMEM((RATIO,), jnp.int32),
            pltpu.SemaphoreType.DMA((7,)),
            pltpu.SemaphoreType.DMA((9, 2)),
            pltpu.SemaphoreType.DMA((10, 2)),
            pltpu.SemaphoreType.DMA((9,)),
            pltpu.SemaphoreType.DMA((9,)),
            pltpu.SemaphoreType.DMA((3, 2)),
            pltpu.SemaphoreType.DMA((3, 2)),
            pltpu.SemaphoreType.DMA((8, 2)),
            pltpu.SemaphoreType.DMA((4, 2, 2)),
            pltpu.SemaphoreType.DMA((2, 2)),
            pltpu.SemaphoreType.DMA((2, 2)),
            pltpu.SemaphoreType.DMA((2,)),
            pltpu.SemaphoreType.DMA((2,)),
        ],
        compiler_params=pltpu.CompilerParams(collective_id=0, has_side_effects=True, vmem_limit_bytes=56 * 1024 * 1024),
    )(slab_order, windows, queries, key_vectors, values, out_proj, grad_out)
    return pl.pallas_call(
        finish,
        name="finish",
        out_shape=tuple(jax.ShapeDtypeStruct(shape, BF) for shape in shapes),
        in_specs=[vmem] * 4,
        out_specs=(hbm,) * 4,
        scratch_shapes=[pltpu.SemaphoreType.DMA((4,))],
        compiler_params=pltpu.CompilerParams(vmem_limit_bytes=8 * 1024 * 1024),
    )(*results)


def solution(mesh):
    in_specs = (
        P("seq", "head"),
        P("seq", "head"),
        P("seq", "head"),
        P("head", None),
        P("seq", "head"),
        P("head"),
        P(),
    )
    out_specs = (P("seq", "head"), P("seq", "head"), P("seq", "head"), P("seq", "head"))
    return jax.shard_map(body, mesh=mesh, in_specs=in_specs, out_specs=out_specs, check_vma=False)
```

```python
import jax
import jax.numpy as jnp
from jax import lax
from jax.experimental import pallas as pl
from jax.experimental.pallas import tpu as pltpu
from jax.sharding import PartitionSpec as P

MESH = pl.DeviceIdType.MESH
BF = jnp.bfloat16
F32 = jnp.float32
ROWS = 256
DIM = 128
RATIO = 4
SCALE = DIM ** (-0.5)
LOG2E = 1.4426950408889634
LOWEST = -1e30
OWN, SPARE = 8, 9


def nn(a, b):
    return jnp.dot(a, b, preferred_element_type=F32)


def nt(a, b):
    return lax.dot_general(a, b, (((1,), (1,)), ((), ())), preferred_element_type=F32)


def kernel(
    order_hbm, spans_hbm, q_hbm, k_hbm, v_hbm, w_hbm, g_hbm,
    out_ref, gq_ref, gk_ref, gv_ref,
    qv, kv, w, gb, qt, qs, st, peak, total, acc, gsum, dos, dot_t, lse, delta, dqt, attn,
    sh_send, sh_f0, sh_part, sh_opp, dsend, drecv, ysend, yrecv, zsend, zrecv, dacc, place, whole, order, spans,
    lsem, c_send, c_recv, a_send, a_recv, b_send, b_recv, d_send, d_recv, y_send, y_recv, z_send, z_recv,
):
    s = lax.axis_index("seq")
    hd = lax.axis_index("head")
    y, x, zl = s // 8, (s // 2) % 4, s % 2
    zh, core = hd // 2, hd % 2
    r = 2 * x + zl
    rp = 2 * x + 1 - zl
    row0 = y * 8
    up = ((y + 1) % 4) * 8
    down = ((y + 3) % 4) * 8
    partner = {"head": 2 * zh + 1 - core}
    opposite = {"head": 2 * (1 - zh) + core}
    q0, q1 = 2 * zh + core, 2 * zh + 1 - core
    f0, f1 = 2 * (1 - zh) + core, 2 * (1 - zh) + 1 - core

    def at_seq(index):
        return {"seq": index}

    def remote(src, dst, send, recv, device):
        return pltpu.make_async_remote_copy(
            src_ref=src, dst_ref=dst, send_sem=send, recv_sem=recv, device_id=device, device_id_type=MESH
        )

    loads = [
        pltpu.make_async_copy(k_hbm, kv.at[OWN, 0], lsem.at[0]),
        pltpu.make_async_copy(v_hbm, kv.at[OWN, 1], lsem.at[1]),
        pltpu.make_async_copy(g_hbm, gb.at[0], lsem.at[2]),
        pltpu.make_async_copy(q_hbm, qv, lsem.at[3]),
        pltpu.make_async_copy(w_hbm, w, lsem.at[4]),
        pltpu.make_async_copy(order_hbm, order, lsem.at[5]),
        pltpu.make_async_copy(spans_hbm, spans, lsem.at[6]),
    ]
    for load in loads:
        load.start()

    barrier = pltpu.get_barrier_semaphore()
    for away in range(1, 4):
        pl.semaphore_signal(barrier, inc=1, device_id=at_seq(row0 + (r + 2 * away) % 8), device_id_type=MESH)
    for device in (at_seq(row0 + rp), partner, opposite, at_seq(up + r), at_seq(down + r)):
        pl.semaphore_signal(barrier, inc=1, device_id=device, device_id_type=MESH)
    edge = jnp.logical_or(x == 0, x == 3)

    @pl.when(edge)
    def _():
        corner = jnp.where(x == 3, up + zl, down + 6 + zl)
        pl.semaphore_signal(barrier, inc=1, device_id=at_seq(corner), device_id_type=MESH)

    pl.semaphore_wait(barrier, jnp.where(edge, 9, 8))

    op_slot = jnp.where(zl == 0, SPARE, r - 1)
    yp_slot = jnp.where(zl == 0, r + 1, SPARE)
    op_there = jnp.where(zl == 1, SPARE, r)

    def kv_copy(src, dst, part, send, device):
        return remote(kv.at[src, part], kv.at[dst, part], c_send, c_recv.at[dst, part], device)

    def side(away, other, part):
        xx = (x + away) % 4
        straight = jnp.logical_and(x == 3, away == 1)
        later = jnp.logical_or(xx > x, straight)
        row = jnp.where(straight, up, row0)
        if other:
            src = jnp.where(later, op_slot, yp_slot)
        else:
            src = jnp.where(later, OWN, r)
        dst = rp if other else r
        return later, kv_copy(src, dst, part, 3 + 2 * (away - 1) + other, at_seq(row + 2 * xx + zl))

    def start_sides(other, later_now, part):
        for away in (2, 1, 3):
            later, copy = side(away, other, part)

            @pl.when(later if later_now else jnp.logical_not(later))
            def _():
                copy.start()

    def own_copy(part, dst, send, device):
        return remote((k_hbm, v_hbm)[part], kv.at[dst, part], c_send, c_recv.at[dst, part], device)

    def to_half(part):
        return own_copy(part, op_there, 0, at_seq(row0 + rp))

    def to_up(part):
        return own_copy(part, r, 1, at_seq(up + r))

    def op_up(part):
        return kv_copy(op_slot, yp_slot, part, 2, at_seq(up + r))

    def await_part(slot, part):
        kv_copy(OWN, slot, part, 0, at_seq(row0 + rp)).wait_recv()

    for part in (0, 1):
        to_half(part).start()
        to_up(part).start()
    for part in (0, 1):
        loads[part].wait()
        start_sides(0, True, part)
    pieces = 4
    piece = ROWS // pieces
    a_opp = [
        remote(gb.at[0, pl.ds(i * piece, piece)], gb.at[2, pl.ds(i * piece, piece)], a_send, a_recv.at[i], opposite)
        for i in range(pieces)
    ]
    a_part = remote(gb.at[0], gb.at[1], a_send, a_recv.at[2 * pieces], partner)
    a_fwd = [
        remote(gb.at[2, pl.ds(i * piece, piece)], gb.at[3, pl.ds(i * piece, piece)], a_send, a_recv.at[pieces + i], partner)
        for i in range(pieces)
    ]
    place[...] = lax.broadcasted_iota(jnp.int32, (ROWS, ROWS), 1) - lax.broadcasted_iota(jnp.int32, (ROWS, ROWS), 0)
    dqt[...] = jnp.zeros_like(dqt)
    dacc[zl, 1] = jnp.zeros((2, ROWS, DIM), F32)
    loads[3].wait()
    for h in range(RATIO):
        block = qv[:, h * DIM : (h + 1) * DIM]
        qs[pl.ds(h * ROWS, ROWS), :] = block
        qt[:, h * ROWS : (h + 1) * ROWS] = block.T
    loads[5].wait()
    loads[6].wait()
    mine = order[s]

    def forward(slot, hidden, first=False):
        key = kv[slot, 0]
        value_t = kv[slot, 1].T
        tops = []
        for h in range(RATIO):
            cols = slice(h * ROWS, (h + 1) * ROWS)
            scores = jnp.where(hidden(h), LOWEST, nn(key, qt[:, cols]) * (SCALE * LOG2E))
            st[slot, :, cols] = scores
            tops.append(jnp.max(scores, axis=0, keepdims=True))
        for h in range(RATIO):
            cols = slice(h * ROWS, (h + 1) * ROWS)
            if first:
                top = tops[h]
                probs = jnp.exp2(st[slot, :, cols] - top)
                total[:, cols] = jnp.sum(probs, axis=0, keepdims=True)
                acc[:, cols] = nn(value_t, probs.astype(BF))
            else:
                before = peak[:, cols]
                top = jnp.maximum(before, tops[h])
                fade = jnp.exp2(before - top)
                probs = jnp.exp2(st[slot, :, cols] - top)
                total[:, cols] = total[:, cols] * fade + jnp.sum(probs, axis=0, keepdims=True)
                acc[:, cols] = acc[:, cols] * fade + nn(value_t, probs.astype(BF))
            peak[:, cols] = top

    def forward_on(slot):
        row = jnp.where(slot < r, row0, down)
        gap = (mine - order[row + slot]) * ROWS

        def windowed(h):
            limit = jnp.where(gap > 0, spans[h] - gap, -100000)
            return place[...] >= limit

        forward(slot, windowed)

    def pair_slot(away, other):
        return 2 * ((x + away) % 4) + (zl + other) % 2

    forward(OWN, lambda h: place[...] < 0, first=True)

    loads[2].wait()
    a_part.start()
    for copy in a_opp:
        copy.start()

    for part in (0, 1):
        await_part(op_slot, part)
        op_up(part).start()
        start_sides(1, True, part)
    def row_before(slot, other, passing):
        @pl.when(x > 0 if passing else x == 0)
        def _():
            for part in (0, 1):
                await_part(slot, part)
                if passing:
                    start_sides(other, False, part)

    row_before(r, 0, True)

    loads[4].wait()

    def w_cols(quarter):
        return pl.ds(pl.multiple_of(quarter * 1024, 1024), 1024)

    gsum[...] = nt(gb[0], w[:, w_cols(q0)])
    a_part.wait_recv()
    gsum[...] += nt(gb[1], w[:, w_cols(q1)])

    def far_columns(group):
        rows = pl.ds(group * 128, 128)
        gsum[rows, :] += nt(gb[2, rows, :], w[:, w_cols(f0)])
        for i in (2 * group, 2 * group + 1):
            a_fwd[i].wait_recv()
        gsum[rows, :] += nt(gb[3, rows, :], w[:, w_cols(f1)])
        for h in range(RATIO):
            grad = gsum[rows, h * DIM : (h + 1) * DIM].astype(BF)
            dos[pl.ds(h * ROWS + group * 128, 128), :] = grad
            dot_t[:, pl.ds(h * ROWS + group * 128, 128)] = grad.T

    row_before(yp_slot, 1, True)

    def pass_on(*which):
        for i in which:
            a_opp[i].wait_recv()
            a_fwd[i].start()

    orders = (
        ((3, 0), (1, 0), 0, (2, 0), 1, (3, 1), (1, 1), (2, 1)),
        (0, 1, (3, 0), (3, 1), (1, 0), (2, 0), (1, 1), (2, 1)),
        (0, 1, (3, 0), (2, 0), (3, 1), (2, 1), (1, 0), (1, 1)),
        (0, 1, (3, 0), (2, 0), (1, 0), (3, 1), (2, 1), (1, 1)),
    )

    def by_x(values):
        return jnp.where(x == 0, values[0], jnp.where(x == 1, values[1], jnp.where(x == 2, values[2], values[3])))

    def slot_of(what):
        if what == 0:
            return r
        return rp if what == 1 else pair_slot(*what)

    def forward_step(i):
        picks = [order_x[i] for order_x in orders]
        slot = by_x([slot_of(what) for what in picks])
        paired = by_x([int(isinstance(what, tuple)) for what in picks])

        @pl.when(paired == 1)
        def _():
            for part in (0, 1):
                await_part(slot, part)

        if i == 2:
            row_before(r, 0, False)
        if i == 4:
            row_before(yp_slot, 1, False)
        forward_on(slot)

    for i in range(3):
        forward_step(i)
    pass_on(0)
    forward_step(3)
    pass_on(1)
    forward_step(4)
    forward_step(5)
    pass_on(2)
    forward_step(6)
    forward_step(7)

    norm = 1.0 / total[...]
    lse[...] = peak[...] + jnp.log(total[...]) * LOG2E
    for h in range(RATIO):
        cols = slice(h * ROWS, (h + 1) * ROWS)
        mixed = (acc[:, cols] * norm[:, cols]).astype(BF)
        attn[:, h * DIM : (h + 1) * DIM] = mixed.T
        acc[:, cols] = mixed.astype(F32)

    def share(quarter, i):
        return nn(attn[...], w[:, pl.ds(pl.multiple_of(quarter * 1024 + i * 512, 512), 512)])

    def b_part(which, i):
        return remote(sh_send.at[which, i], sh_part.at[which, i], b_send, b_recv.at[which, i], partner)

    def b_opp(i):
        return remote(sh_f0.at[i], sh_opp.at[i], b_send, b_recv.at[2, i], opposite)

    def share_out(i):
        b_part(0, i).wait_recv()
        sh_f0[i] = (share(f0, i) + sh_part[0, i].astype(F32)).astype(BF)
        b_opp(i).start()

    pass_on(3)
    for i in range(2):
        sh_send[0, i] = share(f1, i).astype(BF)
        b_part(0, i).start()
    far_columns(0)
    far_columns(1)
    delta[...] = jnp.sum(dot_t[...].astype(F32) * acc[...], axis=0, keepdims=True)

    def backward(slot):
        key_t = kv[slot, 0].T
        value = kv[slot, 1]
        probs_all = []
        grads_all = []
        for h in range(RATIO):
            cols = slice(h * ROWS, (h + 1) * ROWS)
            probs = jnp.exp2(st[slot, :, cols] - lse[:, cols])
            grad_probs = nn(value, dot_t[:, cols])
            probs_all.append(probs.astype(BF))
            grads_all.append((probs * (grad_probs - delta[:, cols])).astype(BF))
        probs_all = jnp.concatenate(probs_all, axis=1)
        grads_all = jnp.concatenate(grads_all, axis=1)
        grad_key = nn(grads_all, qs[...]) * SCALE
        grad_value = nn(probs_all, dos[...])
        dqt[...] += nn(key_t, grads_all)
        return grad_key, grad_value

    def pair_grads(away, other, part):
        slot = pair_slot(away, other)
        return remote(
            dsend.at[slot, part],
            drecv.at[x, other, part],
            d_send,
            d_recv.at[x, other, part],
            at_seq(row0 + 2 * ((x + away) % 4) + zl),
        )

    def turn_away(turn):
        return jnp.where(x == 0, 3 - turn, 2 - turn + 3 * (turn // 2))

    def backward_step(j, carry):
        other = 1 - j // 3
        away = turn_away(j % 3)
        slot = pair_slot(away, other)
        grad_key, grad_value = backward(slot)
        dsend[slot, 0] = grad_key.astype(BF)
        pair_grads(away, other, 0).start()
        dsend[slot, 1] = grad_value.astype(BF)

        @pl.when(other == 1)
        def _():
            pair_grads(away, other, 1).start()

        return carry

    share_out(0)
    lax.fori_loop(0, 2, backward_step, 0)
    share_out(1)
    lax.fori_loop(2, 6, backward_step, 0)
    for turn in range(3):
        pair_grads(turn_away(turn), 0, 1).start()

    def backward_here(slot, row, other):
        grad_key, grad_value = backward(slot)
        dacc[row, other, 0] = grad_key
        dacc[row, other, 1] = grad_value

    backward_here(rp, 1 - zl, 1)
    backward_here(r, 1, 0)

    def pair_from(index, other, part):
        return remote(
            dsend.at[r, part], drecv.at[index, other, part], d_send, d_recv.at[index, other, part], at_seq(row0 + rp)
        )

    def y_copy(other, part):
        return remote(
            ysend.at[other, part], yrecv.at[other, part], y_send, y_recv.at[other, part], at_seq(down + r)
        )

    def z_copy(part):
        return remote(zsend.at[part], zrecv.at[part], z_send, z_recv.at[part], at_seq(row0 + rp))

    def add_from(index, row, other, part):
        pair_from(index, other, part).wait_recv()
        dacc[row, other, part] += drecv[index, other, part].astype(F32)

    def send_up(other, part):
        @pl.loop(0, x)
        def _(index):
            add_from(x - 1 - index, 1, other, part)

        ysend[other, part] = dacc[1, other, part].astype(BF)
        y_copy(other, part).start()

    def add_later(other, part):
        @pl.loop(x + 1, 4)
        def _(index):
            add_from(index, 0, other, part)

    has_other = x + 1 - zl > 0
    backward_here(OWN, 0, 0)
    for i in range(2):
        sh_send[1, i] = share(q1, i).astype(BF)
        b_part(1, i).start()
    for h in range(RATIO):
        gq_ref[:, h * DIM : (h + 1) * DIM] = (dqt[:, h * ROWS : (h + 1) * ROWS] * SCALE).astype(BF).T
    for i in range(2):
        whole[i] = share(q0, i)
    @pl.when(has_other)
    def _():
        for part in (0, 1):
            send_up(1, part)

    for part in (0, 1):
        add_later(1, part)
    send_up(0, 0)
    add_later(0, 0)

    for part in (0, 1):

        @pl.when(has_other)
        def _():
            y_copy(1, part).wait_recv()
            zsend[part] = (dacc[0, 1, part] + yrecv[1, part].astype(F32)).astype(BF)

        @pl.when(jnp.logical_not(has_other))
        def _():
            zsend[part] = dacc[0, 1, part].astype(BF)

        z_copy(part).start()

    send_up(0, 1)
    add_later(0, 1)

    for i in range(2):
        b_part(1, i).wait_recv()
        b_opp(i).wait_recv()
        out_ref[:, i * 512 : (i + 1) * 512] = (whole[i] + sh_part[1, i].astype(F32) + sh_opp[i].astype(F32)).astype(BF)

    def all_left(ref, send, recv):
        remote(ref, ref, send, recv, at_seq(row0 + rp)).wait_send()

    all_left(kv.at[pl.ds(0, 9)], c_send, c_recv.at[0, 0])
    all_left(gb.at[pl.ds(0, 3)], a_send, a_recv.at[0])
    all_left(gb.at[pl.ds(0, 3)], b_send, b_recv.at[0, 0])
    all_left(dsend.at[pl.ds(0, 6)], d_send, d_recv.at[0, 0, 0])
    all_left(zsend, z_send, z_recv.at[0])

    @pl.when(has_other)
    def _():
        all_left(ysend, y_send, y_recv.at[0, 0])

    @pl.when(jnp.logical_not(has_other))
    def _():
        all_left(ysend.at[0], y_send, y_recv.at[0, 0])

    for part, result in ((0, gk_ref), (1, gv_ref)):
        y_copy(0, part).wait_recv()
        z_copy(part).wait_recv()
        result[...] = (dacc[0, 0, part] + yrecv[0, part].astype(F32) + zrecv[part].astype(F32)).astype(BF)


def finish(*refs):
    ins, outs, sems = refs[:4], refs[4:8], refs[8]
    copies = [pltpu.make_async_copy(a, b, sems.at[i]) for i, (a, b) in enumerate(zip(ins, outs))]
    for copy in copies:
        copy.start()
    for copy in copies:
        copy.wait()


def body(queries, key_vectors, values, out_proj, grad_out, windows, slab_order):
    hbm = pl.BlockSpec(memory_space=pltpu.HBM)
    vmem = pl.BlockSpec(memory_space=pltpu.VMEM)
    wide = RATIO * ROWS
    shapes = ((ROWS, 1024), (ROWS, RATIO * DIM), (ROWS, DIM), (ROWS, DIM))
    results = pl.pallas_call(
        kernel,
        name="layer",
        out_shape=tuple(pltpu.VMEM(shape, BF) for shape in shapes),
        in_specs=[hbm] * 7,
        out_specs=(vmem, vmem, vmem, vmem),
        scratch_shapes=[
            pltpu.VMEM((ROWS, RATIO * DIM), BF),
            pltpu.VMEM((10, 2, ROWS, DIM), BF),
            pltpu.VMEM((RATIO * DIM, 4096), BF),
            pltpu.VMEM((4, ROWS, 1024), BF),
            pltpu.VMEM((DIM, wide), BF),
            pltpu.VMEM((wide, DIM), BF),
            pltpu.VMEM((9, ROWS, wide), F32),
            pltpu.VMEM((1, wide), F32),
            pltpu.VMEM((1, wide), F32),
            pltpu.VMEM((DIM, wide), F32),
            pltpu.VMEM((ROWS, RATIO * DIM), F32),
            pltpu.VMEM((wide, DIM), BF),
            pltpu.VMEM((DIM, wide), BF),
            pltpu.VMEM((1, wide), F32),
            pltpu.VMEM((1, wide), F32),
            pltpu.VMEM((DIM, wide), F32),
            pltpu.VMEM((ROWS, RATIO * DIM), BF),
            pltpu.VMEM((2, 2, ROWS, 512), BF),
            pltpu.VMEM((2, ROWS, 512), BF),
            pltpu.VMEM((2, 2, ROWS, 512), BF),
            pltpu.VMEM((2, ROWS, 512), BF),
            pltpu.VMEM((8, 2, ROWS, DIM), BF),
            pltpu.VMEM((4, 2, 2, ROWS, DIM), BF),
            pltpu.VMEM((2, 2, ROWS, DIM), BF),
            pltpu.VMEM((2, 2, ROWS, DIM), BF),
            pltpu.VMEM((2, ROWS, DIM), BF),
            pltpu.VMEM((2, ROWS, DIM), BF),
            pltpu.VMEM((2, 2, 2, ROWS, DIM), F32),
            pltpu.VMEM((ROWS, ROWS), jnp.int32),
            pltpu.VMEM((2, ROWS, 512), F32),
            pltpu.SMEM((32,), jnp.int32),
            pltpu.SMEM((RATIO,), jnp.int32),
            pltpu.SemaphoreType.DMA((7,)),
            pltpu.SemaphoreType.DMA,
            pltpu.SemaphoreType.DMA((10, 2)),
            pltpu.SemaphoreType.DMA,
            pltpu.SemaphoreType.DMA((9,)),
            pltpu.SemaphoreType.DMA,
            pltpu.SemaphoreType.DMA((3, 2)),
            pltpu.SemaphoreType.DMA,
            pltpu.SemaphoreType.DMA((4, 2, 2)),
            pltpu.SemaphoreType.DMA,
            pltpu.SemaphoreType.DMA((2, 2)),
            pltpu.SemaphoreType.DMA,
            pltpu.SemaphoreType.DMA((2,)),
        ],
        compiler_params=pltpu.CompilerParams(collective_id=0, has_side_effects=True, vmem_limit_bytes=56 * 1024 * 1024),
    )(slab_order, windows, queries, key_vectors, values, out_proj, grad_out)
    return pl.pallas_call(
        finish,
        name="finish",
        out_shape=tuple(jax.ShapeDtypeStruct(shape, BF) for shape in shapes),
        in_specs=[vmem] * 4,
        out_specs=(hbm,) * 4,
        scratch_shapes=[pltpu.SemaphoreType.DMA((4,))],
        compiler_params=pltpu.CompilerParams(vmem_limit_bytes=8 * 1024 * 1024),
    )(*results)


def solution(mesh):
    in_specs = (
        P("seq", "head"),
        P("seq", "head"),
        P("seq", "head"),
        P("head", None),
        P("seq", "head"),
        P("head"),
        P(),
    )
    out_specs = (P("seq", "head"), P("seq", "head"), P("seq", "head"), P("seq", "head"))
    return jax.shard_map(body, mesh=mesh, in_specs=in_specs, out_specs=out_specs, check_vma=False)
```

```python
import jax
import jax.numpy as jnp
from jax import lax
from jax.experimental import pallas as pl
from jax.experimental.pallas import tpu as pltpu
from jax.sharding import PartitionSpec as P

MESH = pl.DeviceIdType.MESH
BF = jnp.bfloat16
F32 = jnp.float32
ROWS = 256
DIM = 128
RATIO = 4
SCALE = DIM ** (-0.5)
LOG2E = 1.4426950408889634
LOWEST = -1e30
OWN, SPARE = 8, 9


def nn(a, b):
    return jnp.dot(a, b, preferred_element_type=F32)


def nt(a, b):
    return lax.dot_general(a, b, (((1,), (1,)), ((), ())), preferred_element_type=F32)


def kernel(
    order_hbm, spans_hbm, q_hbm, k_hbm, v_hbm, w_hbm, g_hbm,
    out_ref, gq_ref, gk_ref, gv_ref,
    qv, kv, w, gb, qt, qs, st, peak, total, acc, gsum, dos, dot_t, lse, delta, dqt, attn,
    sh_send, sh_f0, sh_part, sh_opp, dsend, drecv, ysend, yrecv, zsend, zrecv, dacc, place, whole, order, spans,
    lsem, c_send, c_recv, a_send, a_recv, b_send, b_recv, d_send, d_recv, y_send, y_recv, z_send, z_recv,
):
    s = lax.axis_index("seq")
    hd = lax.axis_index("head")
    y, x, zl = s // 8, (s // 2) % 4, s % 2
    zh, core = hd // 2, hd % 2
    r = 2 * x + zl
    rp = 2 * x + 1 - zl
    row0 = y * 8
    up = ((y + 1) % 4) * 8
    down = ((y + 3) % 4) * 8
    partner = {"head": 2 * zh + 1 - core}
    opposite = {"head": 2 * (1 - zh) + core}
    q0, q1 = 2 * zh + core, 2 * zh + 1 - core
    f0, f1 = 2 * (1 - zh) + core, 2 * (1 - zh) + 1 - core

    def at_seq(index):
        return {"seq": index}

    def remote(src, dst, send, recv, device):
        return pltpu.make_async_remote_copy(
            src_ref=src, dst_ref=dst, send_sem=send, recv_sem=recv, device_id=device, device_id_type=MESH
        )

    loads = [
        pltpu.make_async_copy(k_hbm, kv.at[OWN, 0], lsem.at[0]),
        pltpu.make_async_copy(v_hbm, kv.at[OWN, 1], lsem.at[1]),
        pltpu.make_async_copy(g_hbm, gb.at[0], lsem.at[2]),
        pltpu.make_async_copy(q_hbm, qv, lsem.at[3]),
        pltpu.make_async_copy(w_hbm, w, lsem.at[4]),
        pltpu.make_async_copy(order_hbm, order, lsem.at[5]),
        pltpu.make_async_copy(spans_hbm, spans, lsem.at[6]),
    ]
    for load in loads:
        load.start()

    barrier = pltpu.get_barrier_semaphore()
    for away in range(1, 4):
        pl.semaphore_signal(barrier, inc=1, device_id=at_seq(row0 + (r + 2 * away) % 8), device_id_type=MESH)
    for device in (at_seq(row0 + rp), partner, opposite, at_seq(up + r), at_seq(down + r)):
        pl.semaphore_signal(barrier, inc=1, device_id=device, device_id_type=MESH)
    edge = jnp.logical_or(x == 0, x == 3)

    @pl.when(edge)
    def _():
        corner = jnp.where(x == 3, up + zl, down + 6 + zl)
        pl.semaphore_signal(barrier, inc=1, device_id=at_seq(corner), device_id_type=MESH)

    pl.semaphore_wait(barrier, jnp.where(edge, 9, 8))

    op_slot = jnp.where(zl == 0, SPARE, r - 1)
    yp_slot = jnp.where(zl == 0, r + 1, SPARE)
    op_there = jnp.where(zl == 1, SPARE, r)

    def kv_copy(src, dst, part, send, device):
        return remote(kv.at[src, part], kv.at[dst, part], c_send, c_recv.at[dst, part], device)

    def side(away, other, part):
        xx = (x + away) % 4
        straight = jnp.logical_and(x == 3, away == 1)
        later = jnp.logical_or(xx > x, straight)
        row = jnp.where(straight, up, row0)
        if other:
            src = jnp.where(later, op_slot, yp_slot)
        else:
            src = jnp.where(later, OWN, r)
        dst = rp if other else r
        return later, kv_copy(src, dst, part, 3 + 2 * (away - 1) + other, at_seq(row + 2 * xx + zl))

    def start_sides(other, later_now, part):
        for away in (2, 1, 3):
            later, copy = side(away, other, part)

            @pl.when(later if later_now else jnp.logical_not(later))
            def _():
                copy.start()

    def own_copy(part, dst, send, device):
        return remote((k_hbm, v_hbm)[part], kv.at[dst, part], c_send, c_recv.at[dst, part], device)

    def to_half(part):
        return own_copy(part, op_there, 0, at_seq(row0 + rp))

    def to_up(part):
        return own_copy(part, r, 1, at_seq(up + r))

    def op_up(part):
        return kv_copy(op_slot, yp_slot, part, 2, at_seq(up + r))

    def await_part(slot, part):
        kv_copy(OWN, slot, part, 0, at_seq(row0 + rp)).wait_recv()

    for part in (0, 1):
        to_half(part).start()
        to_up(part).start()
    for part in (0, 1):
        loads[part].wait()
        start_sides(0, True, part)
    pieces = 4
    piece = ROWS // pieces
    a_opp = [
        remote(gb.at[0, pl.ds(i * piece, piece)], gb.at[2, pl.ds(i * piece, piece)], a_send, a_recv.at[i], opposite)
        for i in range(pieces)
    ]
    a_part = remote(gb.at[0], gb.at[1], a_send, a_recv.at[2 * pieces], partner)
    a_fwd = [
        remote(gb.at[2, pl.ds(i * piece, piece)], gb.at[3, pl.ds(i * piece, piece)], a_send, a_recv.at[pieces + i], partner)
        for i in range(pieces)
    ]
    place[...] = lax.broadcasted_iota(jnp.int32, (ROWS, ROWS), 1) - lax.broadcasted_iota(jnp.int32, (ROWS, ROWS), 0)
    dqt[...] = jnp.zeros_like(dqt)
    dacc[zl, 1] = jnp.zeros((2, ROWS, DIM), F32)
    loads[3].wait()
    for h in range(RATIO):
        block = qv[:, h * DIM : (h + 1) * DIM]
        qs[pl.ds(h * ROWS, ROWS), :] = block
        qt[:, h * ROWS : (h + 1) * ROWS] = block.T
    loads[5].wait()
    loads[6].wait()
    mine = order[s]

    def forward(slot, hidden, first=False):
        key = kv[slot, 0]
        value_t = kv[slot, 1].T
        tops = []
        for h in range(RATIO):
            cols = slice(h * ROWS, (h + 1) * ROWS)
            scores = jnp.where(hidden(h), LOWEST, nn(key, qt[:, cols]) * (SCALE * LOG2E))
            st[slot, :, cols] = scores
            tops.append(jnp.max(scores, axis=0, keepdims=True))
        for h in range(RATIO):
            cols = slice(h * ROWS, (h + 1) * ROWS)
            if first:
                top = tops[h]
                probs = jnp.exp2(st[slot, :, cols] - top)
                total[:, cols] = jnp.sum(probs, axis=0, keepdims=True)
                acc[:, cols] = nn(value_t, probs.astype(BF))
            else:
                before = peak[:, cols]
                top = jnp.maximum(before, tops[h])
                fade = jnp.exp2(before - top)
                probs = jnp.exp2(st[slot, :, cols] - top)
                total[:, cols] = total[:, cols] * fade + jnp.sum(probs, axis=0, keepdims=True)
                acc[:, cols] = acc[:, cols] * fade + nn(value_t, probs.astype(BF))
            peak[:, cols] = top

    def forward_on(slot):
        row = jnp.where(slot < r, row0, down)
        gap = (mine - order[row + slot]) * ROWS

        def windowed(h):
            limit = jnp.where(gap > 0, spans[h] - gap, -100000)
            return place[...] >= limit

        forward(slot, windowed)

    def pair_slot(away, other):
        return 2 * ((x + away) % 4) + (zl + other) % 2

    forward(OWN, lambda h: place[...] < 0, first=True)

    loads[2].wait()
    a_part.start()
    for copy in a_opp:
        copy.start()

    for part in (0, 1):
        await_part(op_slot, part)
        op_up(part).start()
        start_sides(1, True, part)
    def row_before(slot, other, passing):
        @pl.when(x > 0 if passing else x == 0)
        def _():
            for part in (0, 1):
                await_part(slot, part)
                if passing:
                    start_sides(other, False, part)

    row_before(r, 0, True)

    loads[4].wait()

    def w_cols(quarter):
        return pl.ds(pl.multiple_of(quarter * 1024, 1024), 1024)

    gsum[...] = nt(gb[0], w[:, w_cols(q0)])
    a_part.wait_recv()
    gsum[...] += nt(gb[1], w[:, w_cols(q1)])

    def far_columns(group):
        rows = pl.ds(group * 128, 128)
        gsum[rows, :] += nt(gb[2, rows, :], w[:, w_cols(f0)])
        for i in (2 * group, 2 * group + 1):
            a_fwd[i].wait_recv()
        gsum[rows, :] += nt(gb[3, rows, :], w[:, w_cols(f1)])
        for h in range(RATIO):
            grad = gsum[rows, h * DIM : (h + 1) * DIM].astype(BF)
            dos[pl.ds(h * ROWS + group * 128, 128), :] = grad
            dot_t[:, pl.ds(h * ROWS + group * 128, 128)] = grad.T

    row_before(yp_slot, 1, True)

    def pass_on(*which):
        for i in which:
            a_opp[i].wait_recv()
            a_fwd[i].start()

    orders = (
        ((3, 0), (1, 0), 0, (2, 0), 1, (3, 1), (1, 1), (2, 1)),
        (0, 1, (3, 0), (3, 1), (1, 0), (2, 0), (1, 1), (2, 1)),
        (0, 1, (3, 0), (2, 0), (3, 1), (2, 1), (1, 0), (1, 1)),
        (0, 1, (3, 0), (3, 1), (2, 0), (1, 0), (2, 1), (1, 1)),
    )

    def by_x(values):
        return jnp.where(x == 0, values[0], jnp.where(x == 1, values[1], jnp.where(x == 2, values[2], values[3])))

    def slot_of(what):
        if what == 0:
            return r
        return rp if what == 1 else pair_slot(*what)

    def forward_step(i):
        picks = [order_x[i] for order_x in orders]
        slot = by_x([slot_of(what) for what in picks])
        paired = by_x([int(isinstance(what, tuple)) for what in picks])

        @pl.when(paired == 1)
        def _():
            for part in (0, 1):
                await_part(slot, part)

        if i == 2:
            row_before(r, 0, False)
        if i == 4:
            row_before(yp_slot, 1, False)
        forward_on(slot)

    for i in range(3):
        forward_step(i)
    pass_on(0)
    forward_step(3)
    pass_on(1)
    forward_step(4)
    forward_step(5)
    pass_on(2)
    forward_step(6)
    forward_step(7)

    norm = 1.0 / total[...]
    lse[...] = peak[...] + jnp.log(total[...]) * LOG2E
    for h in range(RATIO):
        cols = slice(h * ROWS, (h + 1) * ROWS)
        mixed = (acc[:, cols] * norm[:, cols]).astype(BF)
        attn[:, h * DIM : (h + 1) * DIM] = mixed.T
        acc[:, cols] = mixed.astype(F32)

    def share(quarter, i):
        return nn(attn[...], w[:, pl.ds(pl.multiple_of(quarter * 1024 + i * 512, 512), 512)])

    def b_part(which, i):
        return remote(sh_send.at[which, i], sh_part.at[which, i], b_send, b_recv.at[which, i], partner)

    def b_opp(i):
        return remote(sh_f0.at[i], sh_opp.at[i], b_send, b_recv.at[2, i], opposite)

    def share_out(i):
        b_part(0, i).wait_recv()
        sh_f0[i] = (share(f0, i) + sh_part[0, i].astype(F32)).astype(BF)
        b_opp(i).start()

    pass_on(3)
    for i in range(2):
        sh_send[0, i] = share(f1, i).astype(BF)
        b_part(0, i).start()
    far_columns(0)
    far_columns(1)
    delta[...] = jnp.sum(dot_t[...].astype(F32) * acc[...], axis=0, keepdims=True)

    def backward(slot):
        key_t = kv[slot, 0].T
        value = kv[slot, 1]
        probs_all = []
        grads_all = []
        for h in range(RATIO):
            cols = slice(h * ROWS, (h + 1) * ROWS)
            probs = jnp.exp2(st[slot, :, cols] - lse[:, cols])
            grad_probs = nn(value, dot_t[:, cols])
            probs_all.append(probs.astype(BF))
            grads_all.append((probs * (grad_probs - delta[:, cols])).astype(BF))
        probs_all = jnp.concatenate(probs_all, axis=1)
        grads_all = jnp.concatenate(grads_all, axis=1)
        grad_key = nn(grads_all, qs[...]) * SCALE
        grad_value = nn(probs_all, dos[...])
        dqt[...] += nn(key_t, grads_all)
        return grad_key, grad_value

    def pair_grads(away, other, part):
        slot = pair_slot(away, other)
        return remote(
            dsend.at[slot, part],
            drecv.at[x, other, part],
            d_send,
            d_recv.at[x, other, part],
            at_seq(row0 + 2 * ((x + away) % 4) + zl),
        )

    def turn_away(turn):
        return jnp.where(x == 0, 3 - turn, 2 - turn + 3 * (turn // 2))

    def backward_step(j, carry):
        other = 1 - j // 3
        away = turn_away(j % 3)
        slot = pair_slot(away, other)
        grad_key, grad_value = backward(slot)
        dsend[slot, 0] = grad_key.astype(BF)
        pair_grads(away, other, 0).start()
        dsend[slot, 1] = grad_value.astype(BF)

        @pl.when(other == 1)
        def _():
            pair_grads(away, other, 1).start()

        return carry

    share_out(0)
    lax.fori_loop(0, 2, backward_step, 0)
    share_out(1)
    lax.fori_loop(2, 6, backward_step, 0)
    for turn in range(3):
        pair_grads(turn_away(turn), 0, 1).start()

    def backward_here(slot, row, other):
        grad_key, grad_value = backward(slot)
        dacc[row, other, 0] = grad_key
        dacc[row, other, 1] = grad_value

    backward_here(rp, 1 - zl, 1)
    backward_here(r, 1, 0)

    def pair_from(index, other, part):
        return remote(
            dsend.at[r, part], drecv.at[index, other, part], d_send, d_recv.at[index, other, part], at_seq(row0 + rp)
        )

    def y_copy(other, part):
        return remote(
            ysend.at[other, part], yrecv.at[other, part], y_send, y_recv.at[other, part], at_seq(down + r)
        )

    def z_copy(part):
        return remote(zsend.at[part], zrecv.at[part], z_send, z_recv.at[part], at_seq(row0 + rp))

    def add_from(index, row, other, part):
        pair_from(index, other, part).wait_recv()
        dacc[row, other, part] += drecv[index, other, part].astype(F32)

    def send_up(other, part):
        @pl.loop(0, x)
        def _(index):
            add_from(x - 1 - index, 1, other, part)

        ysend[other, part] = dacc[1, other, part].astype(BF)
        y_copy(other, part).start()

    def add_later(other, part):
        @pl.loop(x + 1, 4)
        def _(index):
            add_from(index, 0, other, part)

    has_other = x + 1 - zl > 0
    backward_here(OWN, 0, 0)
    for i in range(2):
        sh_send[1, i] = share(q1, i).astype(BF)
        b_part(1, i).start()
    for h in range(RATIO):
        gq_ref[:, h * DIM : (h + 1) * DIM] = (dqt[:, h * ROWS : (h + 1) * ROWS] * SCALE).astype(BF).T
    for i in range(2):
        whole[i] = share(q0, i)
    @pl.when(has_other)
    def _():
        for part in (0, 1):
            send_up(1, part)

    for part in (0, 1):
        add_later(1, part)
    send_up(0, 0)
    add_later(0, 0)

    for part in (0, 1):

        @pl.when(has_other)
        def _():
            y_copy(1, part).wait_recv()
            zsend[part] = (dacc[0, 1, part] + yrecv[1, part].astype(F32)).astype(BF)

        @pl.when(jnp.logical_not(has_other))
        def _():
            zsend[part] = dacc[0, 1, part].astype(BF)

        z_copy(part).start()

    send_up(0, 1)
    add_later(0, 1)

    for i in range(2):
        b_part(1, i).wait_recv()
        b_opp(i).wait_recv()
        out_ref[:, i * 512 : (i + 1) * 512] = (whole[i] + sh_part[1, i].astype(F32) + sh_opp[i].astype(F32)).astype(BF)

    def all_left(ref, send, recv):
        remote(ref, ref, send, recv, at_seq(row0 + rp)).wait_send()

    all_left(kv.at[pl.ds(0, 9)], c_send, c_recv.at[0, 0])
    all_left(gb.at[pl.ds(0, 3)], a_send, a_recv.at[0])
    all_left(gb.at[pl.ds(0, 3)], b_send, b_recv.at[0, 0])
    all_left(dsend.at[pl.ds(0, 6)], d_send, d_recv.at[0, 0, 0])
    all_left(zsend, z_send, z_recv.at[0])

    @pl.when(has_other)
    def _():
        all_left(ysend, y_send, y_recv.at[0, 0])

    @pl.when(jnp.logical_not(has_other))
    def _():
        all_left(ysend.at[0], y_send, y_recv.at[0, 0])

    for part, result in ((0, gk_ref), (1, gv_ref)):
        y_copy(0, part).wait_recv()
        z_copy(part).wait_recv()
        result[...] = (dacc[0, 0, part] + yrecv[0, part].astype(F32) + zrecv[part].astype(F32)).astype(BF)


def finish(*refs):
    ins, outs, sems = refs[:4], refs[4:8], refs[8]
    copies = [pltpu.make_async_copy(a, b, sems.at[i]) for i, (a, b) in enumerate(zip(ins, outs))]
    for copy in copies:
        copy.start()
    for copy in copies:
        copy.wait()


def body(queries, key_vectors, values, out_proj, grad_out, windows, slab_order):
    hbm = pl.BlockSpec(memory_space=pltpu.HBM)
    vmem = pl.BlockSpec(memory_space=pltpu.VMEM)
    wide = RATIO * ROWS
    shapes = ((ROWS, 1024), (ROWS, RATIO * DIM), (ROWS, DIM), (ROWS, DIM))
    results = pl.pallas_call(
        kernel,
        name="layer",
        out_shape=tuple(pltpu.VMEM(shape, BF) for shape in shapes),
        in_specs=[hbm] * 7,
        out_specs=(vmem, vmem, vmem, vmem),
        scratch_shapes=[
            pltpu.VMEM((ROWS, RATIO * DIM), BF),
            pltpu.VMEM((10, 2, ROWS, DIM), BF),
            pltpu.VMEM((RATIO * DIM, 4096), BF),
            pltpu.VMEM((4, ROWS, 1024), BF),
            pltpu.VMEM((DIM, wide), BF),
            pltpu.VMEM((wide, DIM), BF),
            pltpu.VMEM((9, ROWS, wide), F32),
            pltpu.VMEM((1, wide), F32),
            pltpu.VMEM((1, wide), F32),
            pltpu.VMEM((DIM, wide), F32),
            pltpu.VMEM((ROWS, RATIO * DIM), F32),
            pltpu.VMEM((wide, DIM), BF),
            pltpu.VMEM((DIM, wide), BF),
            pltpu.VMEM((1, wide), F32),
            pltpu.VMEM((1, wide), F32),
            pltpu.VMEM((DIM, wide), F32),
            pltpu.VMEM((ROWS, RATIO * DIM), BF),
            pltpu.VMEM((2, 2, ROWS, 512), BF),
            pltpu.VMEM((2, ROWS, 512), BF),
            pltpu.VMEM((2, 2, ROWS, 512), BF),
            pltpu.VMEM((2, ROWS, 512), BF),
            pltpu.VMEM((8, 2, ROWS, DIM), BF),
            pltpu.VMEM((4, 2, 2, ROWS, DIM), BF),
            pltpu.VMEM((2, 2, ROWS, DIM), BF),
            pltpu.VMEM((2, 2, ROWS, DIM), BF),
            pltpu.VMEM((2, ROWS, DIM), BF),
            pltpu.VMEM((2, ROWS, DIM), BF),
            pltpu.VMEM((2, 2, 2, ROWS, DIM), F32),
            pltpu.VMEM((ROWS, ROWS), jnp.int32),
            pltpu.VMEM((2, ROWS, 512), F32),
            pltpu.SMEM((32,), jnp.int32),
            pltpu.SMEM((RATIO,), jnp.int32),
            pltpu.SemaphoreType.DMA((7,)),
            pltpu.SemaphoreType.DMA,
            pltpu.SemaphoreType.DMA((10, 2)),
            pltpu.SemaphoreType.DMA,
            pltpu.SemaphoreType.DMA((9,)),
            pltpu.SemaphoreType.DMA,
            pltpu.SemaphoreType.DMA((3, 2)),
            pltpu.SemaphoreType.DMA,
            pltpu.SemaphoreType.DMA((4, 2, 2)),
            pltpu.SemaphoreType.DMA,
            pltpu.SemaphoreType.DMA((2, 2)),
            pltpu.SemaphoreType.DMA,
            pltpu.SemaphoreType.DMA((2,)),
        ],
        compiler_params=pltpu.CompilerParams(collective_id=0, has_side_effects=True, vmem_limit_bytes=56 * 1024 * 1024),
    )(slab_order, windows, queries, key_vectors, values, out_proj, grad_out)
    return pl.pallas_call(
        finish,
        name="finish",
        out_shape=tuple(jax.ShapeDtypeStruct(shape, BF) for shape in shapes),
        in_specs=[vmem] * 4,
        out_specs=(hbm,) * 4,
        scratch_shapes=[pltpu.SemaphoreType.DMA((4,))],
        compiler_params=pltpu.CompilerParams(vmem_limit_bytes=8 * 1024 * 1024),
    )(*results)


def solution(mesh):
    in_specs = (
        P("seq", "head"),
        P("seq", "head"),
        P("seq", "head"),
        P("head", None),
        P("seq", "head"),
        P("head"),
        P(),
    )
    out_specs = (P("seq", "head"), P("seq", "head"), P("seq", "head"), P("seq", "head"))
    return jax.shard_map(body, mesh=mesh, in_specs=in_specs, out_specs=out_specs, check_vma=False)
```

```python
import jax
import jax.numpy as jnp
from jax import lax
from jax.experimental import pallas as pl
from jax.experimental.pallas import tpu as pltpu
from jax.sharding import PartitionSpec as P

MESH = pl.DeviceIdType.MESH
BF = jnp.bfloat16
F32 = jnp.float32
ROWS = 256
DIM = 128
RATIO = 4
SCALE = DIM ** (-0.5)
LOG2E = 1.4426950408889634
LOWEST = -1e30
OWN, SPARE = 8, 9


def nn(a, b):
    return jnp.dot(a, b, preferred_element_type=F32)


def nt(a, b):
    return lax.dot_general(a, b, (((1,), (1,)), ((), ())), preferred_element_type=F32)


def kernel(
    order_hbm, spans_hbm, q_hbm, k_hbm, v_hbm, w_hbm, g_hbm,
    out_ref, gq_ref, gk_ref, gv_ref,
    qv, kv, w, gb, qt, qs, st, peak, total, acc, gsum, dos, dot_t, lse, delta, dqt, attn,
    sh_send, sh_f0, sh_part, sh_opp, dsend, drecv, ysend, yrecv, zsend, zrecv, dacc, place, whole, order, spans,
    lsem, c_send, c_recv, a_send, a_recv, b_send, b_recv, d_send, d_recv, y_send, y_recv, z_send, z_recv,
):
    s = lax.axis_index("seq")
    hd = lax.axis_index("head")
    y, x, zl = s // 8, (s // 2) % 4, s % 2
    zh, core = hd // 2, hd % 2
    r = 2 * x + zl
    rp = 2 * x + 1 - zl
    row0 = y * 8
    up = ((y + 1) % 4) * 8
    down = ((y + 3) % 4) * 8
    partner = {"head": 2 * zh + 1 - core}
    opposite = {"head": 2 * (1 - zh) + core}
    q0, q1 = 2 * zh + core, 2 * zh + 1 - core
    f0, f1 = 2 * (1 - zh) + core, 2 * (1 - zh) + 1 - core

    def at_seq(index):
        return {"seq": index}

    def remote(src, dst, send, recv, device):
        return pltpu.make_async_remote_copy(
            src_ref=src, dst_ref=dst, send_sem=send, recv_sem=recv, device_id=device, device_id_type=MESH
        )

    loads = [
        pltpu.make_async_copy(k_hbm, kv.at[OWN, 0], lsem.at[0]),
        pltpu.make_async_copy(v_hbm, kv.at[OWN, 1], lsem.at[1]),
        pltpu.make_async_copy(g_hbm, gb.at[0], lsem.at[2]),
        pltpu.make_async_copy(q_hbm, qv, lsem.at[3]),
        pltpu.make_async_copy(w_hbm, w, lsem.at[4]),
        pltpu.make_async_copy(order_hbm, order, lsem.at[5]),
        pltpu.make_async_copy(spans_hbm, spans, lsem.at[6]),
    ]
    for load in loads:
        load.start()

    barrier = pltpu.get_barrier_semaphore()
    for away in range(1, 4):
        pl.semaphore_signal(barrier, inc=1, device_id=at_seq(row0 + (r + 2 * away) % 8), device_id_type=MESH)
    for device in (at_seq(row0 + rp), partner, opposite, at_seq(up + r), at_seq(down + r)):
        pl.semaphore_signal(barrier, inc=1, device_id=device, device_id_type=MESH)
    edge = jnp.logical_or(x == 0, x == 3)

    @pl.when(edge)
    def _():
        corner = jnp.where(x == 3, up + zl, down + 6 + zl)
        pl.semaphore_signal(barrier, inc=1, device_id=at_seq(corner), device_id_type=MESH)

    pl.semaphore_wait(barrier, jnp.where(edge, 9, 8))

    op_slot = jnp.where(zl == 0, SPARE, r - 1)
    yp_slot = jnp.where(zl == 0, r + 1, SPARE)
    op_there = jnp.where(zl == 1, SPARE, r)

    def kv_copy(src, dst, part, send, device):
        return remote(kv.at[src, part], kv.at[dst, part], c_send, c_recv.at[dst, part], device)

    def side(away, other, part):
        xx = (x + away) % 4
        straight = jnp.logical_and(x == 3, away == 1)
        later = jnp.logical_or(xx > x, straight)
        row = jnp.where(straight, up, row0)
        if other:
            src = jnp.where(later, op_slot, yp_slot)
        else:
            src = jnp.where(later, OWN, r)
        dst = rp if other else r
        return later, kv_copy(src, dst, part, 3 + 2 * (away - 1) + other, at_seq(row + 2 * xx + zl))

    def start_sides(other, later_now, part):
        for away in (2, 1, 3):
            later, copy = side(away, other, part)

            @pl.when(later if later_now else jnp.logical_not(later))
            def _():
                copy.start()

    def own_copy(part, dst, send, device):
        return remote((k_hbm, v_hbm)[part], kv.at[dst, part], c_send, c_recv.at[dst, part], device)

    def to_half(part):
        return own_copy(part, op_there, 0, at_seq(row0 + rp))

    def to_up(part):
        return own_copy(part, r, 1, at_seq(up + r))

    def op_up(part):
        return kv_copy(op_slot, yp_slot, part, 2, at_seq(up + r))

    def await_part(slot, part):
        kv_copy(OWN, slot, part, 0, at_seq(row0 + rp)).wait_recv()

    for part in (0, 1):
        to_half(part).start()
        to_up(part).start()
    for part in (0, 1):
        loads[part].wait()
        start_sides(0, True, part)
    pieces = 4
    cuts = (0, 80, 160, 224, ROWS)
    a_opp = [
        remote(gb.at[0, pl.ds(cuts[i], cuts[i + 1] - cuts[i])], gb.at[2, pl.ds(cuts[i], cuts[i + 1] - cuts[i])], a_send, a_recv.at[i], opposite)
        for i in range(pieces)
    ]
    a_part = remote(gb.at[0], gb.at[1], a_send, a_recv.at[2 * pieces], partner)
    a_fwd = [
        remote(gb.at[2, pl.ds(cuts[i], cuts[i + 1] - cuts[i])], gb.at[3, pl.ds(cuts[i], cuts[i + 1] - cuts[i])], a_send, a_recv.at[pieces + i], partner)
        for i in range(pieces)
    ]
    place[...] = lax.broadcasted_iota(jnp.int32, (ROWS, ROWS), 1) - lax.broadcasted_iota(jnp.int32, (ROWS, ROWS), 0)
    dqt[...] = jnp.zeros_like(dqt)
    dacc[zl, 1] = jnp.zeros((2, ROWS, DIM), F32)
    loads[3].wait()
    for h in range(RATIO):
        block = qv[:, h * DIM : (h + 1) * DIM]
        qs[pl.ds(h * ROWS, ROWS), :] = block
        qt[:, h * ROWS : (h + 1) * ROWS] = block.T
    loads[5].wait()
    loads[6].wait()
    mine = order[s]

    def forward(slot, hidden, first=False):
        key = kv[slot, 0]
        value_t = kv[slot, 1].T
        tops = []
        for h in range(RATIO):
            cols = slice(h * ROWS, (h + 1) * ROWS)
            scores = jnp.where(hidden(h), LOWEST, nn(key, qt[:, cols]) * (SCALE * LOG2E))
            st[slot, :, cols] = scores
            tops.append(jnp.max(scores, axis=0, keepdims=True))
        for h in range(RATIO):
            cols = slice(h * ROWS, (h + 1) * ROWS)
            if first:
                top = tops[h]
                probs = jnp.exp2(st[slot, :, cols] - top)
                total[:, cols] = jnp.sum(probs, axis=0, keepdims=True)
                acc[:, cols] = nn(value_t, probs.astype(BF))
            else:
                before = peak[:, cols]
                top = jnp.maximum(before, tops[h])
                fade = jnp.exp2(before - top)
                probs = jnp.exp2(st[slot, :, cols] - top)
                total[:, cols] = total[:, cols] * fade + jnp.sum(probs, axis=0, keepdims=True)
                acc[:, cols] = acc[:, cols] * fade + nn(value_t, probs.astype(BF))
            peak[:, cols] = top

    def forward_on(slot):
        row = jnp.where(slot < r, row0, down)
        gap = (mine - order[row + slot]) * ROWS

        def windowed(h):
            limit = jnp.where(gap > 0, spans[h] - gap, -100000)
            return place[...] >= limit

        forward(slot, windowed)

    def pair_slot(away, other):
        return 2 * ((x + away) % 4) + (zl + other) % 2

    forward(OWN, lambda h: place[...] < 0, first=True)

    loads[2].wait()
    a_part.start()
    for copy in a_opp:
        copy.start()

    for part in (0, 1):
        await_part(op_slot, part)
        op_up(part).start()
        start_sides(1, True, part)
    def row_before(slot, other, passing):
        @pl.when(x > 0 if passing else x == 0)
        def _():
            for part in (0, 1):
                await_part(slot, part)
                if passing:
                    start_sides(other, False, part)

    row_before(r, 0, True)

    loads[4].wait()

    def w_cols(quarter):
        return pl.ds(pl.multiple_of(quarter * 1024, 1024), 1024)

    gsum[...] = nt(gb[0], w[:, w_cols(q0)])
    a_part.wait_recv()
    gsum[...] += nt(gb[1], w[:, w_cols(q1)])

    def far_columns(group):
        rows = pl.ds(group * 128, 128)
        gsum[rows, :] += nt(gb[2, rows, :], w[:, w_cols(f0)])
        for i in (2 * group, 2 * group + 1):
            a_fwd[i].wait_recv()
        gsum[rows, :] += nt(gb[3, rows, :], w[:, w_cols(f1)])
        for h in range(RATIO):
            grad = gsum[rows, h * DIM : (h + 1) * DIM].astype(BF)
            dos[pl.ds(h * ROWS + group * 128, 128), :] = grad
            dot_t[:, pl.ds(h * ROWS + group * 128, 128)] = grad.T

    row_before(yp_slot, 1, True)

    def pass_on(*which):
        for i in which:
            a_opp[i].wait_recv()
            a_fwd[i].start()

    orders = (
        ((3, 0), (1, 0), 0, (2, 0), 1, (3, 1), (1, 1), (2, 1)),
        (0, 1, (3, 0), (3, 1), (1, 0), (2, 0), (1, 1), (2, 1)),
        (0, 1, (3, 0), (2, 0), (3, 1), (2, 1), (1, 0), (1, 1)),
        (0, 1, (3, 0), (2, 0), (1, 0), (3, 1), (2, 1), (1, 1)),
    )

    def by_x(values):
        return jnp.where(x == 0, values[0], jnp.where(x == 1, values[1], jnp.where(x == 2, values[2], values[3])))

    def slot_of(what):
        if what == 0:
            return r
        return rp if what == 1 else pair_slot(*what)

    def forward_step(i):
        picks = [order_x[i] for order_x in orders]
        slot = by_x([slot_of(what) for what in picks])
        paired = by_x([int(isinstance(what, tuple)) for what in picks])

        @pl.when(paired == 1)
        def _():
            for part in (0, 1):
                await_part(slot, part)

        if i == 2:
            row_before(r, 0, False)
        if i == 4:
            row_before(yp_slot, 1, False)
        forward_on(slot)

    for i in range(3):
        forward_step(i)
    pass_on(0)
    forward_step(3)
    pass_on(1)
    forward_step(4)
    forward_step(5)
    pass_on(2)
    forward_step(6)
    forward_step(7)

    norm = 1.0 / total[...]
    lse[...] = peak[...] + jnp.log(total[...]) * LOG2E
    for h in range(RATIO):
        cols = slice(h * ROWS, (h + 1) * ROWS)
        mixed = (acc[:, cols] * norm[:, cols]).astype(BF)
        attn[:, h * DIM : (h + 1) * DIM] = mixed.T
        acc[:, cols] = mixed.astype(F32)

    def share(quarter, i):
        return nn(attn[...], w[:, pl.ds(pl.multiple_of(quarter * 1024 + i * 512, 512), 512)])

    def b_part(which, i):
        return remote(sh_send.at[which, i], sh_part.at[which, i], b_send, b_recv.at[which, i], partner)

    def b_opp(i):
        return remote(sh_f0.at[i], sh_opp.at[i], b_send, b_recv.at[2, i], opposite)

    def share_out(i):
        b_part(0, i).wait_recv()
        sh_f0[i] = (share(f0, i) + sh_part[0, i].astype(F32)).astype(BF)
        b_opp(i).start()

    pass_on(3)
    for i in range(2):
        sh_send[0, i] = share(f1, i).astype(BF)
        b_part(0, i).start()
    far_columns(0)
    far_columns(1)
    delta[...] = jnp.sum(dot_t[...].astype(F32) * acc[...], axis=0, keepdims=True)

    def backward(slot):
        key_t = kv[slot, 0].T
        value = kv[slot, 1]
        probs_all = []
        grads_all = []
        for h in range(RATIO):
            cols = slice(h * ROWS, (h + 1) * ROWS)
            probs = jnp.exp2(st[slot, :, cols] - lse[:, cols])
            grad_probs = nn(value, dot_t[:, cols])
            probs_all.append(probs.astype(BF))
            grads_all.append((probs * (grad_probs - delta[:, cols])).astype(BF))
        probs_all = jnp.concatenate(probs_all, axis=1)
        grads_all = jnp.concatenate(grads_all, axis=1)
        grad_key = nn(grads_all, qs[...]) * SCALE
        grad_value = nn(probs_all, dos[...])
        dqt[...] += nn(key_t, grads_all)
        return grad_key, grad_value

    def pair_grads(away, other, part):
        slot = pair_slot(away, other)
        return remote(
            dsend.at[slot, part],
            drecv.at[x, other, part],
            d_send,
            d_recv.at[x, other, part],
            at_seq(row0 + 2 * ((x + away) % 4) + zl),
        )

    def turn_away(turn):
        return jnp.where(x == 0, 3 - turn, 2 - turn + 3 * (turn // 2))

    def backward_step(j, carry):
        other = 1 - j // 3
        away = turn_away(j % 3)
        slot = pair_slot(away, other)
        grad_key, grad_value = backward(slot)
        dsend[slot, 0] = grad_key.astype(BF)
        pair_grads(away, other, 0).start()
        dsend[slot, 1] = grad_value.astype(BF)

        @pl.when(other == 1)
        def _():
            pair_grads(away, other, 1).start()

        return carry

    share_out(0)
    lax.fori_loop(0, 2, backward_step, 0)
    share_out(1)
    lax.fori_loop(2, 6, backward_step, 0)
    for turn in range(3):
        pair_grads(turn_away(turn), 0, 1).start()

    def backward_here(slot, row, other):
        grad_key, grad_value = backward(slot)
        dacc[row, other, 0] = grad_key
        dacc[row, other, 1] = grad_value

    backward_here(rp, 1 - zl, 1)
    backward_here(r, 1, 0)

    def pair_from(index, other, part):
        return remote(
            dsend.at[r, part], drecv.at[index, other, part], d_send, d_recv.at[index, other, part], at_seq(row0 + rp)
        )

    def y_copy(other, part):
        return remote(
            ysend.at[other, part], yrecv.at[other, part], y_send, y_recv.at[other, part], at_seq(down + r)
        )

    def z_copy(part):
        return remote(zsend.at[part], zrecv.at[part], z_send, z_recv.at[part], at_seq(row0 + rp))

    def add_from(index, row, other, part):
        pair_from(index, other, part).wait_recv()
        dacc[row, other, part] += drecv[index, other, part].astype(F32)

    def send_up(other, part):
        @pl.loop(0, x)
        def _(index):
            add_from(x - 1 - index, 1, other, part)

        ysend[other, part] = dacc[1, other, part].astype(BF)
        y_copy(other, part).start()

    def add_later(other, part):
        @pl.loop(x + 1, 4)
        def _(index):
            add_from(index, 0, other, part)

    has_other = x + 1 - zl > 0
    backward_here(OWN, 0, 0)
    for i in range(2):
        sh_send[1, i] = share(q1, i).astype(BF)
        b_part(1, i).start()
    for h in range(RATIO):
        gq_ref[:, h * DIM : (h + 1) * DIM] = (dqt[:, h * ROWS : (h + 1) * ROWS] * SCALE).astype(BF).T
    for i in range(2):
        whole[i] = share(q0, i)
    @pl.when(has_other)
    def _():
        for part in (0, 1):
            send_up(1, part)

    for part in (0, 1):
        add_later(1, part)
    send_up(0, 0)
    add_later(0, 0)

    for part in (0, 1):

        @pl.when(has_other)
        def _():
            y_copy(1, part).wait_recv()
            zsend[part] = (dacc[0, 1, part] + yrecv[1, part].astype(F32)).astype(BF)

        @pl.when(jnp.logical_not(has_other))
        def _():
            zsend[part] = dacc[0, 1, part].astype(BF)

        z_copy(part).start()

    send_up(0, 1)
    add_later(0, 1)

    for i in range(2):
        b_part(1, i).wait_recv()
        b_opp(i).wait_recv()
        out_ref[:, i * 512 : (i + 1) * 512] = (whole[i] + sh_part[1, i].astype(F32) + sh_opp[i].astype(F32)).astype(BF)

    def all_left(ref, send, recv):
        remote(ref, ref, send, recv, at_seq(row0 + rp)).wait_send()

    all_left(kv.at[pl.ds(0, 9)], c_send, c_recv.at[0, 0])
    all_left(gb.at[pl.ds(0, 3)], a_send, a_recv.at[0])
    all_left(gb.at[pl.ds(0, 3)], b_send, b_recv.at[0, 0])
    all_left(dsend.at[pl.ds(0, 6)], d_send, d_recv.at[0, 0, 0])
    all_left(zsend, z_send, z_recv.at[0])

    @pl.when(has_other)
    def _():
        all_left(ysend, y_send, y_recv.at[0, 0])

    @pl.when(jnp.logical_not(has_other))
    def _():
        all_left(ysend.at[0], y_send, y_recv.at[0, 0])

    for part, result in ((0, gk_ref), (1, gv_ref)):
        y_copy(0, part).wait_recv()
        z_copy(part).wait_recv()
        result[...] = (dacc[0, 0, part] + yrecv[0, part].astype(F32) + zrecv[part].astype(F32)).astype(BF)


def finish(*refs):
    ins, outs, sems = refs[:4], refs[4:8], refs[8]
    copies = [pltpu.make_async_copy(a, b, sems.at[i]) for i, (a, b) in enumerate(zip(ins, outs))]
    for copy in copies:
        copy.start()
    for copy in copies:
        copy.wait()


def body(queries, key_vectors, values, out_proj, grad_out, windows, slab_order):
    hbm = pl.BlockSpec(memory_space=pltpu.HBM)
    vmem = pl.BlockSpec(memory_space=pltpu.VMEM)
    wide = RATIO * ROWS
    shapes = ((ROWS, 1024), (ROWS, RATIO * DIM), (ROWS, DIM), (ROWS, DIM))
    results = pl.pallas_call(
        kernel,
        name="layer",
        out_shape=tuple(pltpu.VMEM(shape, BF) for shape in shapes),
        in_specs=[hbm] * 7,
        out_specs=(vmem, vmem, vmem, vmem),
        scratch_shapes=[
            pltpu.VMEM((ROWS, RATIO * DIM), BF),
            pltpu.VMEM((10, 2, ROWS, DIM), BF),
            pltpu.VMEM((RATIO * DIM, 4096), BF),
            pltpu.VMEM((4, ROWS, 1024), BF),
            pltpu.VMEM((DIM, wide), BF),
            pltpu.VMEM((wide, DIM), BF),
            pltpu.VMEM((9, ROWS, wide), F32),
            pltpu.VMEM((1, wide), F32),
            pltpu.VMEM((1, wide), F32),
            pltpu.VMEM((DIM, wide), F32),
            pltpu.VMEM((ROWS, RATIO * DIM), F32),
            pltpu.VMEM((wide, DIM), BF),
            pltpu.VMEM((DIM, wide), BF),
            pltpu.VMEM((1, wide), F32),
            pltpu.VMEM((1, wide), F32),
            pltpu.VMEM((DIM, wide), F32),
            pltpu.VMEM((ROWS, RATIO * DIM), BF),
            pltpu.VMEM((2, 2, ROWS, 512), BF),
            pltpu.VMEM((2, ROWS, 512), BF),
            pltpu.VMEM((2, 2, ROWS, 512), BF),
            pltpu.VMEM((2, ROWS, 512), BF),
            pltpu.VMEM((8, 2, ROWS, DIM), BF),
            pltpu.VMEM((4, 2, 2, ROWS, DIM), BF),
            pltpu.VMEM((2, 2, ROWS, DIM), BF),
            pltpu.VMEM((2, 2, ROWS, DIM), BF),
            pltpu.VMEM((2, ROWS, DIM), BF),
            pltpu.VMEM((2, ROWS, DIM), BF),
            pltpu.VMEM((2, 2, 2, ROWS, DIM), F32),
            pltpu.VMEM((ROWS, ROWS), jnp.int32),
            pltpu.VMEM((2, ROWS, 512), F32),
            pltpu.SMEM((32,), jnp.int32),
            pltpu.SMEM((RATIO,), jnp.int32),
            pltpu.SemaphoreType.DMA((7,)),
            pltpu.SemaphoreType.DMA,
            pltpu.SemaphoreType.DMA((10, 2)),
            pltpu.SemaphoreType.DMA,
            pltpu.SemaphoreType.DMA((9,)),
            pltpu.SemaphoreType.DMA,
            pltpu.SemaphoreType.DMA((3, 2)),
            pltpu.SemaphoreType.DMA,
            pltpu.SemaphoreType.DMA((4, 2, 2)),
            pltpu.SemaphoreType.DMA,
            pltpu.SemaphoreType.DMA((2, 2)),
            pltpu.SemaphoreType.DMA,
            pltpu.SemaphoreType.DMA((2,)),
        ],
        compiler_params=pltpu.CompilerParams(collective_id=0, has_side_effects=True, vmem_limit_bytes=56 * 1024 * 1024),
    )(slab_order, windows, queries, key_vectors, values, out_proj, grad_out)
    return pl.pallas_call(
        finish,
        name="finish",
        out_shape=tuple(jax.ShapeDtypeStruct(shape, BF) for shape in shapes),
        in_specs=[vmem] * 4,
        out_specs=(hbm,) * 4,
        scratch_shapes=[pltpu.SemaphoreType.DMA((4,))],
        compiler_params=pltpu.CompilerParams(vmem_limit_bytes=8 * 1024 * 1024),
    )(*results)


def solution(mesh):
    in_specs = (
        P("seq", "head"),
        P("seq", "head"),
        P("seq", "head"),
        P("head", None),
        P("seq", "head"),
        P("head"),
        P(),
    )
    out_specs = (P("seq", "head"), P("seq", "head"), P("seq", "head"), P("seq", "head"))
    return jax.shard_map(body, mesh=mesh, in_specs=in_specs, out_specs=out_specs, check_vma=False)
```
